512 devices in a mesh: space: 256 (over y, z, x), feat: 2 (over core).
Axes of the slice: x: 4, y: 4, z: 16, core: 2. Of those that a mesh axis runs over, the one named last changes fastest.
Arguments:
- nodes: bfloat16 [40960, 512], P('space'), may hold values from -6 to 6
- edges: bfloat16 [196608, 512], P(('space', 'feat')), may hold values from -6 to 6
- senders: int32 [196608], P(('space', 'feat')), may hold values from 0 to 40959, as said below
- receivers: int32 [196608], P(('space', 'feat')), may hold values from 0 to 40959, as said below
- edge_proj: bfloat16 [512, 512], replicated, may hold values from -0.15625 to 0.15625
- send_proj: bfloat16 [512, 512], replicated, may hold values from -0.15625 to 0.15625
- recv_proj: bfloat16 [512, 512], replicated, may hold values from -0.15625 to 0.15625
- edge_bias: float32 [512], replicated, may hold values from -3 to 3
- edge_out: bfloat16 [512, 512], replicated, may hold values from -0.25 to 0.25
- edge_gain: float32 [512], replicated, may hold values from 0.25 to 1.75
- edge_shift: float32 [512], replicated, may hold values from -3 to 3
- node_in: bfloat16 [1024, 512], replicated, may hold values from -0.1875 to 0.1875
- node_bias: float32 [512], replicated, may hold values from -3 to 3
- node_out: bfloat16 [512, 512], replicated, may hold values from -0.25 to 0.25
- node_gain: float32 [512], replicated, may hold values from 0.25 to 1.75
- node_shift: float32 [512], replicated, may hold values from -3 to 3
- node_cot: bfloat16 [40960, 512], P('space'), may hold values from -6 to 6
Outputs:
- new_nodes: bfloat16 [40960, 512], P('space')
- node_grad: bfloat16 [40960, 512], P('space')
- edge_grad: bfloat16 [196608, 512], P(('space', 'feat'))
The draws below stay inside these ranges and needn't reach their ends.
Inputs may be any that keep to these rules, and one draw needn't show every extreme that they name: `senders`: every edge of a block's 768 has its receiver in that block; its sender lies in the same block, in the last 48 rows of the previous block, in the first 48 rows of the next block, or among the first 2 rows of any block. `receivers`: every edge of a block's 768 has its receiver among that block's 160 nodes.
All inputs are finite; a program needn't handle non-finite values.
Results may differ from the reference program's by a relative error of at most 0.0077.
Values may be sent and summed in bfloat16 or wider, within the bound.
No kernel may reach another device: no remote copies, remote signals or barrier semaphores. Data moves between devices by JAX's collectives and lax.ppermute only.
A program may use at most 64 MiB of HBM per device.

```python
import jax
import jax.numpy as jnp
from jax import lax

D = 512
NODE_DEV = 160
EDGE_DEV = 768
RIM = 48
HUB_DEV = 2
NODES = 40960
EDGES = 196608


def draw_senders(key, part):
    blocks = NODES // NODE_DEV
    subkeys = jax.random.split(key, 5)
    position = jnp.arange(EDGES, dtype=jnp.int32)
    owner_block = position // EDGE_DEV
    category = jax.random.randint(subkeys[0], (EDGES,), 0, 5)
    own_row = jax.random.randint(subkeys[1], (EDGES,), 0, NODE_DEV)
    rim_row = jax.random.randint(subkeys[2], (EDGES,), 0, RIM)
    hub_block = jax.random.randint(subkeys[3], (EDGES,), 0, blocks)
    hub_row = jax.random.randint(subkeys[4], (EDGES,), 0, HUB_DEV)
    own_id = owner_block * NODE_DEV + own_row
    left_id = jnp.where(owner_block > 0, (owner_block - 1) * NODE_DEV + NODE_DEV - RIM + rim_row, own_id)
    right_id = jnp.where(owner_block < blocks - 1, (owner_block + 1) * NODE_DEV + rim_row, own_id)
    hub_id = hub_block * NODE_DEV + hub_row
    chosen = jnp.where(category == 2, left_id, jnp.where(category == 3, right_id, jnp.where(category == 4, hub_id, own_id)))
    chosen = jnp.where(position == 0, 0, chosen)
    chosen = jnp.where(position == EDGES - 1, NODES - 1, chosen)
    return chosen.astype(jnp.int32)


def draw_receivers(key, part):
    folded = jax.random.fold_in(key, 7)
    position = jnp.arange(EDGES, dtype=jnp.int32)
    owner_block = position // EDGE_DEV
    own_row = jax.random.randint(folded, (EDGES,), 0, NODE_DEV)
    own_row = jnp.where(position == 0, 0, own_row)
    own_row = jnp.where(position == EDGES - 1, NODE_DEV - 1, own_row)
    return (owner_block * NODE_DEV + own_row).astype(jnp.int32)


def levels(key, shape, shards, smallest, high):
    level, own = 1.0, jax.random.fold_in(key, 6)
    for dim, shards_of in shards:
        draws = jnp.exp(jax.random.uniform(jax.random.fold_in(own, dim), (shards_of,), jnp.float32, smallest / len(shards), high / len(shards)))
        level = level * jnp.repeat(draws, shape[dim] // shards_of).reshape([-1 if axis == dim else 1 for axis in range(len(shape))])
    return level


def bell_draw(rng, dims, scale, reach, shards=(), kind=jnp.bfloat16):
    values = scale * jax.random.normal(rng, dims, jnp.float32)
    if shards:
        values = values * levels(rng, dims, shards, -0.22, 0.18)
    return jnp.clip(values, -reach, reach).astype(kind)


def setup_inputs(seed: int = 0) -> dict:
    keys = jax.random.split(jax.random.key(seed), 18)
    return {
        "nodes": bell_draw(keys[0], (NODES, D), 1.0, 6.0, ((0, 256),)),
        "edges": bell_draw(keys[1], (EDGES, D), 1.0, 6.0, ((0, 512),)),
        "senders": draw_senders(jax.random.fold_in(keys[17], 71), 0),
        "receivers": draw_receivers(jax.random.fold_in(keys[17], 71), 0),
        "edge_proj": bell_draw(keys[4], (D, D), (3 * D) ** -0.5, 0.15625),
        "send_proj": bell_draw(keys[5], (D, D), (3 * D) ** -0.5, 0.15625),
        "recv_proj": bell_draw(keys[6], (D, D), (3 * D) ** -0.5, 0.15625),
        "edge_bias": bell_draw(keys[7], (D,), 0.5, 3.0, (), jnp.float32),
        "edge_out": bell_draw(keys[8], (D, D), D ** -0.5, 0.25),
        "edge_gain": jnp.clip(1.0 + 0.15 * jax.random.normal(keys[9], (D,), jnp.float32), 0.25, 1.75),
        "edge_shift": bell_draw(keys[10], (D,), 0.5, 3.0, (), jnp.float32),
        "node_in": bell_draw(keys[11], (2 * D, D), (2 * D) ** -0.5, 0.1875),
        "node_bias": bell_draw(keys[12], (D,), 0.5, 3.0, (), jnp.float32),
        "node_out": bell_draw(keys[13], (D, D), D ** -0.5, 0.25),
        "node_gain": jnp.clip(1.0 + 0.15 * jax.random.normal(keys[14], (D,), jnp.float32), 0.25, 1.75),
        "node_shift": bell_draw(keys[15], (D,), 0.5, 3.0, (), jnp.float32),
        "node_cot": bell_draw(keys[16], (NODES, D), 1.0, 6.0, ((0, 256),)),
    }


epsilon = 1e-05

def layer_stats(values):
    average = lax.optimization_barrier(jnp.mean(values, axis=-1, keepdims=True))
    centred = values - average
    inv_scale = lax.rsqrt(lax.optimization_barrier(jnp.mean(centred * centred, axis=-1, keepdims=True)) + epsilon)
    return (centred * inv_scale, inv_scale)

def norm_back(upstream, normed, inv_scale, gain_vec):
    scaled = upstream * gain_vec
    return inv_scale * (scaled - lax.optimization_barrier(jnp.mean(scaled, axis=-1, keepdims=True)) - normed * lax.optimization_barrier(jnp.mean(scaled * normed, axis=-1, keepdims=True)))

def swish_slope(preact):
    sigmoid_val = jax.nn.sigmoid(preact)
    return sigmoid_val * (1.0 + preact * (1.0 - sigmoid_val))

def reference(nodes, edges, senders, receivers, edge_proj, send_proj, recv_proj, edge_bias, edge_out, edge_gain, edge_shift, node_in, node_bias, node_out, node_gain, node_shift, node_cot):
    width = nodes.shape[1]
    node_total = nodes.shape[0]
    send_terms = jnp.dot(nodes, send_proj, preferred_element_type=jnp.float32).astype(jnp.bfloat16)
    recv_terms = jnp.dot(nodes, recv_proj, preferred_element_type=jnp.float32).astype(jnp.bfloat16)
    hidden_pre = jnp.dot(edges, edge_proj, preferred_element_type=jnp.float32) + jnp.take(send_terms, senders, axis=0).astype(jnp.float32) + jnp.take(recv_terms, receivers, axis=0).astype(jnp.float32) + edge_bias
    hidden_act = jax.nn.silu(hidden_pre).astype(jnp.bfloat16)
    edge_sum = jnp.dot(hidden_act, edge_out, preferred_element_type=jnp.float32)
    edge_normed, edge_scale = layer_stats(edge_sum)
    new_edges = (edges.astype(jnp.float32) + edge_normed * edge_gain + edge_shift).astype(jnp.bfloat16)
    gathered = jax.ops.segment_sum(new_edges.astype(jnp.float32), receivers, num_segments=node_total).astype(jnp.bfloat16)
    node_pre = jnp.dot(nodes, node_in[:width], preferred_element_type=jnp.float32) + jnp.dot(gathered, node_in[width:], preferred_element_type=jnp.float32) + node_bias
    node_act = jax.nn.silu(node_pre).astype(jnp.bfloat16)
    node_mix = jnp.dot(node_act, node_out, preferred_element_type=jnp.float32)
    node_normed, node_scale = layer_stats(node_mix)
    new_nodes = (nodes.astype(jnp.float32) + node_normed * node_gain + node_shift).astype(jnp.bfloat16)
    upstream = node_cot.astype(jnp.float32)
    node_dmix = norm_back(upstream, node_normed, node_scale, node_gain).astype(jnp.bfloat16)
    node_dact = jnp.dot(node_dmix, node_out.T, preferred_element_type=jnp.float32)
    node_dpre = (node_dact * swish_slope(node_pre)).astype(jnp.bfloat16)
    node_direct = upstream + jnp.dot(node_dpre, node_in[:width].T, preferred_element_type=jnp.float32)
    gathered_grad = jnp.dot(node_dpre, node_in[width:].T, preferred_element_type=jnp.float32)
    edge_upstream = jnp.take(gathered_grad, receivers, axis=0)
    edge_dsum = norm_back(edge_upstream, edge_normed, edge_scale, edge_gain).astype(jnp.bfloat16)
    edge_dact = jnp.dot(edge_dsum, edge_out.T, preferred_element_type=jnp.float32)
    edge_dpre = (edge_dact * swish_slope(hidden_pre)).astype(jnp.bfloat16)
    edge_grad = (edge_upstream + jnp.dot(edge_dpre, edge_proj.T, preferred_element_type=jnp.float32)).astype(jnp.bfloat16)
    send_sums = jax.ops.segment_sum(edge_dpre.astype(jnp.float32), senders, num_segments=node_total)
    recv_sums = jax.ops.segment_sum(edge_dpre.astype(jnp.float32), receivers, num_segments=node_total)
    send_part = jnp.dot(send_sums, send_proj.astype(jnp.float32).T, precision=lax.Precision.HIGHEST)
    recv_part = jnp.dot(recv_sums, recv_proj.astype(jnp.float32).T, precision=lax.Precision.HIGHEST)
    node_grad = (node_direct + send_part + recv_part).astype(jnp.bfloat16)
    return (new_nodes, node_grad, edge_grad)
```

```python
import math

import jax
import jax.numpy as jnp
import numpy as np
from jax import lax
from jax.sharding import Mesh, PartitionSpec as P

RIM = 48
HUB_DEV = 2
EPS = 1e-05
BF = jnp.bfloat16
F32 = jnp.float32
ALL = ("y", "z", "x", "c")
SPACE = ("y", "z", "x")
PLANE = ("y", "x", "c")


def dot(a, b):
    return jnp.dot(a, b, preferred_element_type=F32)


def dot_t(a, b):
    return lax.dot_general(a, b, (((1,), (1,)), ((), ())), preferred_element_type=F32)


def col_sums(onehot, values):
    return lax.dot_general(onehot, values, (((0,), (0,)), ((), ())), preferred_element_type=F32)


def split2(v):
    high = v.astype(BF)
    return high, (v - high.astype(F32)).astype(BF)


def layer_stats(values):
    average = jnp.mean(values, axis=-1, keepdims=True)
    centred = values - average
    inv_scale = lax.rsqrt(jnp.mean(centred * centred, axis=-1, keepdims=True) + EPS)
    return centred * inv_scale, inv_scale


def norm_back(upstream, normed, inv_scale, gain_vec):
    scaled = upstream * gain_vec
    return inv_scale * (
        scaled
        - jnp.mean(scaled, axis=-1, keepdims=True)
        - normed * jnp.mean(scaled * normed, axis=-1, keepdims=True)
    )


def swish_slope(preact):
    sigmoid_val = jax.nn.sigmoid(preact)
    return sigmoid_val * (1.0 + preact * (1.0 - sigmoid_val))


def along_space(x, step):
    count = math.prod(lax.axis_size(a) for a in SPACE)
    return lax.ppermute(x, SPACE, [(i, (i + step) % count) for i in range(count)])


def other_core(x):
    return lax.ppermute(x, "c", [(0, 1), (1, 0)])


def body(
    nodes,
    edges,
    senders,
    receivers,
    edge_proj,
    send_proj,
    recv_proj,
    edge_bias,
    edge_out,
    edge_gain,
    edge_shift,
    node_in,
    node_bias,
    node_out,
    node_gain,
    node_shift,
    node_cot,
):
    node_count, width = nodes.shape
    ny, nz, nx = (lax.axis_size(a) for a in SPACE)
    plane = ny * nx * HUB_DEV
    core = lax.axis_index("c")
    own_block = lax.axis_index(SPACE)
    hub_base = 2 * RIM + node_count
    slots = hub_base + plane * nz

    left_rows = along_space(nodes[node_count - RIM :], 1)
    right_rows = along_space(nodes[:RIM], -1)
    my_hub = lax.dynamic_slice_in_dim(nodes, core, 1, 0).astype(F32)
    by_z = lax.all_to_all(jnp.broadcast_to(my_hub[None], (nz, 1, width)), "z", 0, 0)
    by_z = by_z.reshape(nz, width).astype(BF)
    hubs = lax.all_to_all(jnp.broadcast_to(by_z[None], (plane, nz, width)), PLANE, 0, 0)
    hubs = hubs.reshape(plane * nz, width)

    block = senders // node_count
    row = senders - block * node_count
    hub_y, hub_zx = block // (nz * nx), block % (nz * nx)
    hub_z, hub_x = hub_zx // nx, hub_zx % nx
    hub_slot = ((hub_y * nx + hub_x) * HUB_DEV + row) * nz + hub_z
    slot = jnp.where(
        block == own_block,
        RIM + row,
        jnp.where(
            (block == own_block - 1) & (row >= node_count - RIM),
            row - (node_count - RIM),
            jnp.where(
                (block == own_block + 1) & (row < RIM),
                RIM + node_count + row,
                hub_base + hub_slot,
            ),
        ),
    )
    slot_hot = (slot[:, None] == jnp.arange(slots, dtype=jnp.int32)[None, :]).astype(BF)
    local_recv = receivers - own_block * node_count
    recv_hot = (local_recv[:, None] == jnp.arange(node_count, dtype=jnp.int32)[None, :]).astype(BF)

    table = jnp.concatenate([left_rows, nodes, right_rows, hubs], axis=0)
    send_terms = dot(table, send_proj).astype(BF)
    recv_terms = dot(nodes, recv_proj).astype(BF)
    hidden_pre = (
        dot(edges, edge_proj) + dot(slot_hot, send_terms) + dot(recv_hot, recv_terms) + edge_bias
    )
    hidden_act = jax.nn.silu(hidden_pre).astype(BF)
    edge_normed, edge_scale = layer_stats(dot(hidden_act, edge_out))
    new_edges = (edges.astype(F32) + edge_normed * edge_gain + edge_shift).astype(BF)
    gathered = col_sums(recv_hot, new_edges)
    gathered = (gathered + other_core(gathered)).astype(BF)

    node_pre = dot(nodes, node_in[:width]) + dot(gathered, node_in[width:]) + node_bias
    node_act = jax.nn.silu(node_pre).astype(BF)
    node_normed, node_scale = layer_stats(dot(node_act, node_out))
    new_nodes = (nodes.astype(F32) + node_normed * node_gain + node_shift).astype(BF)
    upstream = node_cot.astype(F32)
    node_dmix = norm_back(upstream, node_normed, node_scale, node_gain).astype(BF)
    node_dpre = (dot_t(node_dmix, node_out) * swish_slope(node_pre)).astype(BF)
    node_direct = upstream + dot_t(node_dpre, node_in[:width])
    gathered_grad = dot_t(node_dpre, node_in[width:])

    grad_high, grad_low = split2(gathered_grad)
    edge_upstream = dot(recv_hot, grad_high) + dot(recv_hot, grad_low)
    edge_dsum = norm_back(edge_upstream, edge_normed, edge_scale, edge_gain).astype(BF)
    edge_dpre = (dot_t(edge_dsum, edge_out) * swish_slope(hidden_pre)).astype(BF)
    slot_sums = col_sums(slot_hot, edge_dpre)
    recv_sums = col_sums(recv_hot, edge_dpre)
    edge_grad = (edge_upstream + dot_t(edge_dpre, edge_proj)).astype(BF)

    back_right = along_space(slot_sums[:RIM].astype(BF), -1)
    back_left = along_space(slot_sums[RIM + node_count : hub_base].astype(BF), 1)
    hub_sums = slot_sums[hub_base:].astype(BF).reshape(plane, nz, width)
    hub_sums = lax.all_to_all(hub_sums, PLANE, 0, 0).astype(F32).sum(0)
    hub_sums = lax.all_to_all(hub_sums.reshape(nz, 1, width), "z", 0, 0).sum(0)
    own_sums = slot_sums[RIM : RIM + node_count]
    own_sums = own_sums + jnp.pad(back_left.astype(F32), ((0, node_count - RIM), (0, 0)))
    own_sums = own_sums + jnp.pad(back_right.astype(F32), ((node_count - RIM, 0), (0, 0)))
    hub_row = (jnp.arange(node_count, dtype=jnp.int32) == core)[:, None]
    own_sums = own_sums + jnp.where(hub_row, hub_sums, 0.0)
    send_high, send_low = split2(own_sums)
    recv_high, recv_low = split2(recv_sums)
    extra = (
        dot_t(send_high, send_proj)
        + dot_t(send_low, send_proj)
        + dot_t(recv_high, recv_proj)
        + dot_t(recv_low, recv_proj)
    )
    extra = extra + other_core(extra)
    node_grad = (node_direct + extra).astype(BF)
    return new_nodes, node_grad, edge_grad


def solution(mesh):
    ny, nz, nx = SHAPE
    fine = Mesh(np.asarray(mesh.devices).reshape(ny, nz, nx, 2), ALL)
    rows, both = P(SPACE, None), P(ALL, None)
    whole = P()
    in_specs = (rows, both, P(ALL), P(ALL)) + (whole,) * 12 + (rows,)
    return jax.shard_map(
        body, mesh=fine, in_specs=in_specs, out_specs=(rows, rows, both), check_vma=False
    )


SHAPE = (4, 16, 4)
```

```python
import functools
import math

import jax
import jax.numpy as jnp
import numpy as np
from jax import lax
from jax.experimental import pallas as pl
from jax.experimental.pallas import tpu as pltpu
from jax.sharding import Mesh, PartitionSpec as P

RIM = 48
HUB_DEV = 2
EPS = 1e-05
BF = jnp.bfloat16
F32 = jnp.float32
I32 = jnp.int32
ALL = ("y", "z", "x", "c")
SPACE = ("y", "z", "x")
PLANE = ("y", "x")
LANES = 128
TILE = 256
SHAPE = (4, 16, 4)


def dot(a, b):
    return jnp.dot(a, b, preferred_element_type=F32)


def dot_t(a, b):
    return lax.dot_general(a, b, (((1,), (1,)), ((), ())), preferred_element_type=F32)


def split2(v):
    high = v.astype(BF)
    return high, (v - high.astype(F32)).astype(BF)


def row_mean(v):
    return jnp.mean(v, axis=-1, keepdims=True)


def layer_stats(values):
    centred = values - row_mean(values)
    inv_scale = lax.rsqrt(row_mean(centred * centred) + EPS)
    return centred * inv_scale, inv_scale


def norm_back(upstream, normed, inv_scale, gain_vec):
    scaled = upstream * gain_vec
    return inv_scale * (scaled - row_mean(scaled) - normed * row_mean(scaled * normed))


def hot_rows(ids, first, count):
    edges = ids.shape[1]
    column = jnp.broadcast_to(ids - first, (LANES, edges)).T
    lane = lax.broadcasted_iota(I32, (edges, LANES), 1)
    parts = [
        jnp.where(column == lane + k, 1.0, 0.0).astype(BF) for k in range(0, count, LANES)
    ]
    return jnp.concatenate(parts, axis=1)[:, :count]


def hot_cols(ids, first, count):
    edges = ids.shape[1]
    slot = lax.broadcasted_iota(I32, (count, edges), 0)
    return jnp.where(slot == ids - first, 1.0, 0.0).astype(BF)


def vmem_call(kernel, outs, args, scratch=(), smem=0, flops=0, name=None):
    spec = pl.BlockSpec(memory_space=pltpu.VMEM)
    ins = [pl.BlockSpec(memory_space=pltpu.SMEM)] * smem + [spec] * (len(args) - smem)
    moved = sum(math.prod(o.shape) * o.dtype.itemsize for o in outs)
    moved += sum(math.prod(a.shape) * a.dtype.itemsize for a in args)
    return pl.pallas_call(
        kernel,
        out_shape=outs,
        in_specs=ins,
        out_specs=[spec] * len(outs),
        scratch_shapes=list(scratch),
        compiler_params=pltpu.CompilerParams(vmem_limit_bytes=40 * 2**20),
        cost_estimate=pl.CostEstimate(flops=flops, bytes_accessed=moved, transcendentals=0),
        name=name,
    )(*args)


def spread_kernel(rows_ref, out_ref):
    nz = rows_ref.shape[0] // 8
    parts = []
    for r in range(HUB_DEV):
        lanes = [rows_ref[pl.ds(4 * r + j, nz, stride=8), :] for j in range(4)]
        parts.append(jnp.concatenate(lanes, axis=1))
    rows = jnp.concatenate(parts, axis=0).astype(BF)
    for p in range(out_ref.shape[0]):
        out_ref[p] = rows


def gather_kernel(sums_ref, out_ref):
    nz = out_ref.shape[0] // 8
    total = sums_ref[0].astype(F32)
    for p in range(1, sums_ref.shape[0]):
        total += sums_ref[p].astype(F32)
    for r in range(HUB_DEV):
        for j in range(4):
            out_ref[pl.ds(4 * r + j, nz, stride=8), :] = total[
                r * nz : (r + 1) * nz, j * LANES : (j + 1) * LANES
            ]


def near_kernel(
    edges_ref, ids_ref, nodes_ref, left_ref, right_ref, we_ref, ws_ref, wr_ref, bias_ref,
    pre_ref, frame_ref, send_ref, recv_ref,
):
    node_count = nodes_ref.shape[0]
    slots = 2 * RIM + node_count
    frame_ref[:RIM] = left_ref[...]
    frame_ref[RIM : RIM + node_count] = nodes_ref[...]
    frame_ref[RIM + node_count :] = right_ref[...]
    send_ref[...] = dot(frame_ref[...], ws_ref[...]).astype(BF)
    recv_ref[...] = dot(frame_ref[...], wr_ref[...]).astype(BF)

    def step(i, carry):
        rows = pl.ds(pl.multiple_of(i * TILE, TILE), TILE)
        pre = dot(edges_ref[rows, :], we_ref[...])
        pre += dot(hot_rows(ids_ref[0:1, rows], 0, slots), send_ref[...])
        pre += dot(hot_rows(ids_ref[1:2, rows], 0, slots), recv_ref[...])
        pre_ref[rows, :] = pre + bias_ref[...]
        return carry

    lax.fori_loop(0, edges_ref.shape[0] // TILE, step, 0)


def main_kernel(
    hubs_ref, pre_ref, edges_ref, ids_ref, nodes_ref, cot_ref, ws_ref, wo_ref, win_ref, wout_ref,
    egain_ref, eshift_ref, nbias_ref, ngain_ref, nshift_ref,
    new_ref, dpre_ref, hub_sums_ref, rim_l_ref, rim_r_ref, own_ref, gg_ref, ndpre_ref,
    terms_ref, slope_ref, normed_ref, scale_ref, gathered_ref, high_ref, low_ref,
):
    node_count, width = nodes_ref.shape
    hub_count = hubs_ref.shape[0]
    edge_count = edges_ref.shape[0]
    slots = 2 * RIM + node_count
    own = slice(RIM, RIM + node_count)
    terms_ref[...] = dot(hubs_ref[...], ws_ref[...]).astype(BF)
    gathered_ref[...] = jnp.zeros_like(gathered_ref)

    def forward(i, carry):
        rows = pl.ds(pl.multiple_of(i * TILE, TILE), TILE)
        pre = pre_ref[rows, :] + dot(hot_rows(ids_ref[0:1, rows], slots, hub_count), terms_ref[...])
        gate = jax.nn.sigmoid(pre)
        slope_ref[rows, :] = gate * (1.0 + pre * (1.0 - gate))
        edge_sum = dot((pre * gate).astype(BF), wo_ref[...])
        normed, scale = layer_stats(edge_sum)
        normed_ref[rows, :] = normed
        scale_ref[rows, :] = jnp.broadcast_to(scale, (TILE, LANES))
        new_edges = edges_ref[rows, :].astype(F32) + normed * egain_ref[...] + eshift_ref[...]
        gathered_ref[...] += dot(hot_cols(ids_ref[1:2, rows], 0, slots), new_edges.astype(BF))
        return carry

    lax.fori_loop(0, edge_count // TILE, forward, 0)

    nodes = nodes_ref[...]
    gathered = gathered_ref[own].astype(BF)
    node_pre = dot(nodes, win_ref[:width]) + dot(gathered, win_ref[width:]) + nbias_ref[...]
    gate = jax.nn.sigmoid(node_pre)
    node_mix = dot((node_pre * gate).astype(BF), wout_ref[...])
    normed, scale = layer_stats(node_mix)
    new_nodes = nodes.astype(F32) + normed * ngain_ref[...] + nshift_ref[...]
    new_ref[...] = new_nodes.astype(BF)
    dmix = norm_back(cot_ref[...].astype(F32), normed, scale, ngain_ref[...]).astype(BF)
    ndpre = dot_t(dmix, wout_ref[...]) * (gate * (1.0 + node_pre * (1.0 - gate)))
    ndpre = ndpre.astype(BF)
    ndpre_ref[...] = ndpre
    gathered_grad = dot_t(ndpre, win_ref[width:])
    gg_ref[...] = gathered_grad
    high, low = split2(gathered_grad)
    for ref, part in ((high_ref, high), (low_ref, low)):
        ref[...] = jnp.zeros_like(ref)
        ref[own] = part

    def backward(i, carry):
        rows = pl.ds(pl.multiple_of(i * TILE, TILE), TILE)
        hot = hot_rows(ids_ref[1:2, rows], 0, slots)
        upstream = dot(hot, high_ref[...]) + dot(hot, low_ref[...])
        dsum = norm_back(upstream, normed_ref[rows, :], scale_ref[rows, :1], egain_ref[...])
        dpre_ref[rows, :] = (dot_t(dsum.astype(BF), wo_ref[...]) * slope_ref[rows, :]).astype(BF)
        return carry

    lax.fori_loop(0, edge_count // TILE, backward, 0)

    dpre = dpre_ref[...]
    hub_sums_ref[...] = dot(hot_cols(ids_ref[0:1, :], slots, hub_count), dpre).astype(BF)
    frame = dot(hot_cols(ids_ref[0:1, :], 0, slots), dpre)
    rim_l_ref[...] = frame[:RIM].astype(BF)
    rim_r_ref[...] = frame[RIM + node_count :].astype(BF)
    own_ref[...] = frame[own]


def late_kernel(
    core_ref, dpre_ref, ids_ref, gg_ref, ndpre_ref, own_ref, cot_ref, we_ref, ws_ref, wr_ref, win_ref,
    egrad_ref, base_ref, high_ref, low_ref,
):
    node_count, width = cot_ref.shape
    slots = 2 * RIM + node_count
    own = slice(RIM, RIM + node_count)
    half = egrad_ref.shape[0]
    high, low = split2(gg_ref[...])
    for ref, part in ((high_ref, high), (low_ref, low)):
        ref[...] = jnp.zeros_like(ref)
        ref[own] = part
    rows = pl.ds(pl.multiple_of(core_ref[0] * half, half), half)
    hot = hot_rows(ids_ref[1:2, rows], 0, slots)
    upstream = dot(hot, high_ref[...]) + dot(hot, low_ref[...])
    egrad_ref[...] = (upstream + dot_t(dpre_ref[rows, :], we_ref[...])).astype(BF)
    base = cot_ref[...].astype(F32) + dot_t(ndpre_ref[...], win_ref[:width])
    recv = dot(hot_cols(ids_ref[1:2, :], RIM, node_count), dpre_ref[...])
    for sums, weight in ((own_ref[...], ws_ref), (recv, wr_ref)):
        high, low = split2(sums)
        base += dot_t(high, weight[...]) + dot_t(low, weight[...])
    base_ref[...] = base


def last_kernel(hub_ref, first_ref, final_ref, base_ref, ws_ref, out_ref, sums_ref):
    node_count = base_ref.shape[0]
    hub = hub_ref[0]
    for z in range(1, hub_ref.shape[0]):
        hub += hub_ref[z]
    rows = [
        jnp.concatenate([hub[4 * r + j : 4 * r + j + 1] for j in range(4)], axis=1)
        for r in range(HUB_DEV)
    ]
    sums_ref[...] = jnp.zeros_like(sums_ref)
    sums_ref[:RIM] = first_ref[...].astype(F32)
    for r in range(HUB_DEV):
        sums_ref[r : r + 1] += rows[r]
    sums_ref[node_count - RIM :] += final_ref[...].astype(F32)
    high, low = split2(sums_ref[...])
    extra = dot_t(high, ws_ref[...]) + dot_t(low, ws_ref[...])
    out_ref[...] = (base_ref[...] + extra).astype(BF)


def along_space(x, step):
    count = math.prod(lax.axis_size(a) for a in SPACE)
    pairs = [(i, i + step) for i in range(count) if 0 <= i + step < count]
    return lax.ppermute(x, SPACE, pairs)


def body(
    nodes,
    edges,
    senders,
    receivers,
    edge_proj,
    send_proj,
    recv_proj,
    edge_bias,
    edge_out,
    edge_gain,
    edge_shift,
    node_in,
    node_bias,
    node_out,
    node_gain,
    node_shift,
    node_cot,
):
    shape = jax.ShapeDtypeStruct
    node_count, width = nodes.shape
    ny, nz, nx = (lax.axis_size(a) for a in SPACE)
    plane = ny * nx
    hub_count = plane * HUB_DEV * nz
    slots = 2 * RIM + node_count
    core = lax.axis_index("c")
    own_block = lax.axis_index(SPACE)
    row = lambda v: v.reshape(1, width)

    my_hub = nodes[:HUB_DEV].astype(F32).reshape(1, 8, LANES)
    by_z = lax.all_to_all(jnp.broadcast_to(my_hub, (nz, 8, LANES)), "z", 0, 0)
    left_rows = along_space(nodes[node_count - RIM :], 1)
    right_rows = along_space(nodes[:RIM], -1)
    (spread,) = vmem_call(
        spread_kernel,
        [shape((plane, HUB_DEV * nz, width), BF)],
        [by_z.reshape(nz * 8, LANES)],
        name="spread",
    )
    hubs = lax.all_to_all(spread, PLANE, 0, 0).reshape(hub_count, width)

    all_edges = lax.all_gather(edges, "c", axis=0, tiled=True)
    ids = lax.all_gather(jnp.stack([senders, receivers]), "c", axis=1, tiled=True)
    edge_count = all_edges.shape[0]
    block = ids[0] // node_count
    line = ids[0] - block * node_count
    hub_y, hub_zx = block // (nz * nx), block % (nz * nx)
    hub_z, hub_x = hub_zx // nx, hub_zx % nx
    hub_slot = ((hub_y * nx + hub_x) * HUB_DEV + line) * nz + hub_z
    slot = jnp.where(
        block == own_block,
        RIM + line,
        jnp.where(
            (block == own_block - 1) & (line >= node_count - RIM),
            line - (node_count - RIM),
            jnp.where(
                (block == own_block + 1) & (line < RIM),
                RIM + node_count + line,
                slots + hub_slot,
            ),
        ),
    )
    ids = jnp.stack([slot, ids[1] - own_block * node_count + RIM])

    square = 2 * width * width
    (near,) = vmem_call(
        near_kernel,
        [shape((edge_count, width), F32)],
        [all_edges, ids, nodes, left_rows, right_rows, edge_proj, send_proj, recv_proj, row(edge_bias)],
        [pltpu.VMEM((slots, width), BF)] * 3,
        flops=square * (edge_count * 2 + 2 * slots),
        name="near",
    )
    new_nodes, dpre, hub_sums, rim_l, rim_r, own_sums, gathered_grad, node_dpre = vmem_call(
        main_kernel,
        [
            shape((node_count, width), BF),
            shape((edge_count, width), BF),
            shape((hub_count, width), BF),
            shape((RIM, width), BF),
            shape((RIM, width), BF),
            shape((node_count, width), F32),
            shape((node_count, width), F32),
            shape((node_count, width), BF),
        ],
        [
            hubs, near, all_edges, ids, nodes, node_cot, send_proj, edge_out, node_in, node_out,
            row(edge_gain), row(edge_shift), row(node_bias), row(node_gain), row(node_shift),
        ],
        [
            pltpu.VMEM((hub_count, width), BF),
            pltpu.VMEM((edge_count, width), F32),
            pltpu.VMEM((edge_count, width), F32),
            pltpu.VMEM((edge_count, LANES), F32),
            pltpu.VMEM((slots, width), F32),
            pltpu.VMEM((slots, width), BF),
            pltpu.VMEM((slots, width), BF),
        ],
        flops=square * (edge_count * 6 + hub_count),
        name="main",
    )

    hub_back = lax.all_to_all(hub_sums.reshape(plane, HUB_DEV * nz, width), PLANE, 0, 0)
    final_back = along_space(rim_l, -1)
    first_back = along_space(rim_r, 1)
    (by_z,) = vmem_call(
        gather_kernel, [shape((nz * 8, LANES), F32)], [hub_back], name="gather"
    )
    hub_back = lax.all_to_all(by_z.reshape(nz, 8, LANES), "z", 0, 0)
    edge_grad, base = vmem_call(
        late_kernel,
        [shape(edges.shape, BF), shape((node_count, width), F32)],
        [
            core.astype(I32).reshape(1), dpre, ids, gathered_grad, node_dpre, own_sums, node_cot,
            edge_proj, send_proj, recv_proj, node_in,
        ],
        [pltpu.VMEM((slots, width), BF)] * 2,
        smem=1,
        flops=square * edge_count * 2,
        name="late",
    )
    (node_grad,) = vmem_call(
        last_kernel,
        [shape((node_count, width), BF)],
        [hub_back, first_back, final_back, base, send_proj],
        [pltpu.VMEM((node_count, width), F32)],
        flops=square * node_count * 2,
        name="last",
    )
    return new_nodes, node_grad, edge_grad


def solution(mesh):
    fine = Mesh(np.asarray(mesh.devices).reshape(*SHAPE, 2), ALL)
    rows, both = P(SPACE, None), P(ALL, None)
    whole = P()
    in_specs = (rows, both, P(ALL), P(ALL)) + (whole,) * 12 + (rows,)
    return jax.shard_map(
        body, mesh=fine, in_specs=in_specs, out_specs=(rows, rows, both), check_vma=False
    )
```

```python
import functools
import math

import jax
import jax.numpy as jnp
import numpy as np
from jax import lax
from jax.experimental import pallas as pl
from jax.experimental.pallas import tpu as pltpu
from jax.sharding import Mesh, PartitionSpec as P

RIM = 48
HUB_DEV = 2
EPS = 1e-05
BF = jnp.bfloat16
F32 = jnp.float32
I32 = jnp.int32
ALL = ("y", "z", "x", "c")
SPACE = ("y", "z", "x")
PLANE = ("y", "x")
LANES = 128
TILE = 256
SHAPE = (4, 16, 4)
GRANT = 60 * 1024 * 1024


def dot(a, b):
    return jnp.dot(a, b, preferred_element_type=F32)


def dot_t(a, b):
    return lax.dot_general(a, b, (((1,), (1,)), ((), ())), preferred_element_type=F32)


def split2(v):
    high = v.astype(BF)
    return high, (v - high.astype(F32)).astype(BF)


def row_mean(v):
    return jnp.mean(v, axis=-1, keepdims=True)


def layer_stats(values):
    centred = values - row_mean(values)
    inv_scale = lax.rsqrt(row_mean(centred * centred) + EPS)
    return centred * inv_scale, inv_scale


def norm_back(upstream, normed, inv_scale, gain_vec):
    scaled = upstream * gain_vec
    return inv_scale * (scaled - row_mean(scaled) - normed * row_mean(scaled * normed))


def hot_rows(ids, first, count):
    edges = ids.shape[1]
    column = jnp.broadcast_to(ids - first, (LANES, edges)).T
    lane = lax.broadcasted_iota(I32, (edges, LANES), 1)
    parts = [
        jnp.where(column == lane + k, 1.0, 0.0).astype(BF) for k in range(0, count, LANES)
    ]
    return jnp.concatenate(parts, axis=1)[:, :count]


def hot_cols(ids, first, count):
    edges = ids.shape[1]
    slot = lax.broadcasted_iota(I32, (count, edges), 0)
    return jnp.where(slot == ids - first, 1.0, 0.0).astype(BF)


VM = pl.BlockSpec(memory_space=pltpu.VMEM)
SM = pl.BlockSpec(memory_space=pltpu.SMEM)
HB = pl.BlockSpec(memory_space=pltpu.HBM)


def call(kernel, ins, outs, scratch=(), copies=0, flops=0, room=0, name=None):
    shapes = [jax.ShapeDtypeStruct(s, d) for s, d, _ in outs]
    args = [a for a, _ in ins]
    moved = sum(math.prod(o.shape) * o.dtype.itemsize for o in shapes + args)
    scratch = list(scratch)
    if copies:
        scratch.append(pltpu.SemaphoreType.DMA((copies,)))
    return pl.pallas_call(
        kernel,
        out_shape=shapes,
        in_specs=[spec for _, spec in ins],
        out_specs=[spec for _, _, spec in outs],
        scratch_shapes=scratch,
        compiler_params=pltpu.CompilerParams(vmem_limit_bytes=GRANT - room * 1024),
        cost_estimate=pl.CostEstimate(flops=flops, bytes_accessed=moved, transcendentals=0),
        name=name,
    )(*args)


def start_copies(pairs, sems, first=0):
    copies = [
        pltpu.make_async_copy(src, dst, sems.at[first + k]) for k, (src, dst) in enumerate(pairs)
    ]
    for copy in copies:
        copy.start()
    return copies


def prep_kernel(core_ref, nodes_ref, hub_ref, rim_ref, head_ref, sems):
    node_count = nodes_ref.shape[0]
    start = pl.multiple_of((1 - core_ref[0]) * (node_count - RIM), 16)
    head, rim = start_copies(
        [(nodes_ref.at[:16], head_ref), (nodes_ref.at[pl.ds(start, RIM)], rim_ref)], sems
    )
    head.wait()
    rows = head_ref[...].astype(F32)
    tile = jnp.concatenate(
        [rows[r : r + 1, j * LANES : (j + 1) * LANES] for r in range(HUB_DEV) for j in range(4)],
        axis=0,
    )
    for z in range(hub_ref.shape[0]):
        hub_ref[z] = tile
    rim.wait()


def spread_kernel(rows_ref, out_ref):
    nz = rows_ref.shape[0] // 8
    parts = []
    for r in range(HUB_DEV):
        lanes = [rows_ref[pl.ds(4 * r + j, nz, stride=8), :] for j in range(4)]
        parts.append(jnp.concatenate(lanes, axis=1))
    rows = jnp.concatenate(parts, axis=0).astype(BF)
    for p in range(out_ref.shape[0]):
        out_ref[p] = rows


def gather_kernel(sums_ref, rim_ref, flag_ref, out_ref, rim_out_ref, buf_ref, sems):
    del flag_ref
    planes = sums_ref.shape[0]
    nz = out_ref.shape[0] // 8
    quarter = planes // 4
    pairs = [
        (sums_ref.at[pl.ds(k * quarter, quarter)], buf_ref.at[pl.ds(k * quarter, quarter)])
        for k in range(4)
    ]
    *copies, rim = start_copies(pairs + [(rim_ref, rim_out_ref)], sems)
    total = jnp.zeros(buf_ref.shape[1:], F32)
    for p in range(planes):
        if p % quarter == 0:
            copies[p // quarter].wait()
        total += buf_ref[p].astype(F32)
    for r in range(HUB_DEV):
        for j in range(4):
            out_ref[pl.ds(4 * r + j, nz, stride=8), :] = total[
                r * nz : (r + 1) * nz, j * LANES : (j + 1) * LANES
            ]
    rim.wait()


def near_kernel(
    edges_in, ids_ref, nodes_in, rims_in, we_in, ws_in, wr_in, bias_ref,
    pre_out,
    edges_ref, frame_ref, we_ref, ws_ref, wr_ref, send_ref, recv_ref, pre_ref, sems,
):
    node_count = nodes_in.shape[0]
    slots = 2 * RIM + node_count
    copies = start_copies(
        [
            (nodes_in, frame_ref.at[pl.ds(RIM, node_count)]),
            (rims_in.at[pl.ds(0, RIM)], frame_ref.at[pl.ds(0, RIM)]),
            (rims_in.at[pl.ds(RIM, RIM)], frame_ref.at[pl.ds(RIM + node_count, RIM)]),
            (ws_in, ws_ref),
            (wr_in, wr_ref),
            (we_in, we_ref),
            (edges_in, edges_ref),
        ],
        sems,
    )
    for copy in copies[:4]:
        copy.wait()
    send_ref[...] = dot(frame_ref[...], ws_ref[...]).astype(BF)
    copies[4].wait()
    recv_ref[...] = dot(frame_ref[...], wr_ref[...]).astype(BF)
    copies[5].wait()
    copies[6].wait()
    back = []
    for i in range(edges_in.shape[0] // TILE):
        rows = pl.ds(i * TILE, TILE)
        pre = dot(edges_ref[rows, :], we_ref[...])
        pre += dot(hot_rows(ids_ref[0:1, rows], 0, slots), send_ref[...])
        pre += dot(hot_rows(ids_ref[1:2, rows], 0, slots), recv_ref[...])
        pre_ref[rows, :] = pre + bias_ref[...]
        back += start_copies([(pre_ref.at[rows], pre_out.at[rows])], sems, 7 + i)
    for copy in back:
        copy.wait()


def main_kernel(
    core_ref, hubs_in, pre_in, edges_in, ids_ref, nodes_in, cot_in, ws_in, wo_in, win_in, wout_in,
    egain_ref, eshift_ref, nbias_ref, ngain_ref, nshift_ref,
    new_ref, dpre_out, hub_sums_out, rim_ref, own_out, gg_out, ndpre_out,
    hubs_ref, pre_ref, edges_ref, nodes_ref, cot_ref, ws_ref, wo_ref, win_ref, wout_ref,
    dpre_ref, hub_sums_ref, gg_ref, ndpre_ref,
    terms_ref, normed_ref, scale_ref, gathered_ref, high_ref, low_ref, sems,
):
    node_count, width = nodes_in.shape
    hub_count = hubs_in.shape[0]
    edge_count = edges_in.shape[0]
    steps = edge_count // TILE
    slots = 2 * RIM + node_count
    own = slice(RIM, RIM + node_count)
    tiles = [pl.ds(i * TILE, TILE) for i in range(steps)]
    hubs, ws, wo, nodes, cot, win, wout, *rest = start_copies(
        [
            (hubs_in, hubs_ref),
            (ws_in, ws_ref),
            (wo_in, wo_ref),
            (nodes_in, nodes_ref),
            (cot_in, cot_ref),
            (win_in, win_ref),
            (wout_in, wout_ref),
        ]
        + [(pre_in.at[rows], pre_ref.at[rows]) for rows in tiles]
        + [(edges_in.at[rows], edges_ref.at[rows]) for rows in tiles],
        sems,
    )
    done = 7 + 2 * steps
    gathered_ref[...] = jnp.zeros_like(gathered_ref)
    hubs.wait()
    ws.wait()
    terms_ref[...] = dot(hubs_ref[...], ws_ref[...]).astype(BF)
    wo.wait()
    for copy in rest:
        copy.wait()

    def forward(i, carry):
        rows = pl.ds(pl.multiple_of(i * TILE, TILE), TILE)
        pre = pre_ref[rows, :] + dot(hot_rows(ids_ref[0:1, rows], slots, hub_count), terms_ref[...])
        gate = jax.nn.sigmoid(pre)
        pre_ref[rows, :] = gate * (1.0 + pre * (1.0 - gate))
        edge_sum = dot((pre * gate).astype(BF), wo_ref[...])
        normed, scale = layer_stats(edge_sum)
        normed_ref[rows, :] = normed
        scale_ref[rows, :] = jnp.broadcast_to(scale, (TILE, LANES))
        new_edges = edges_ref[rows, :].astype(F32) + normed * egain_ref[...] + eshift_ref[...]
        gathered_ref[...] += dot(hot_cols(ids_ref[1:2, rows], 0, slots), new_edges.astype(BF))
        return carry

    lax.fori_loop(0, steps, forward, 0)

    for copy in (nodes, cot, win, wout):
        copy.wait()
    nodes = nodes_ref[...]
    gathered = gathered_ref[own].astype(BF)
    node_pre = dot(nodes, win_ref[:width]) + dot(gathered, win_ref[width:]) + nbias_ref[...]
    gate = jax.nn.sigmoid(node_pre)
    node_mix = dot((node_pre * gate).astype(BF), wout_ref[...])
    normed, scale = layer_stats(node_mix)
    new_nodes = nodes.astype(F32) + normed * ngain_ref[...] + nshift_ref[...]
    new_ref[...] = new_nodes.astype(BF)
    dmix = norm_back(cot_ref[...].astype(F32), normed, scale, ngain_ref[...]).astype(BF)
    ndpre = dot_t(dmix, wout_ref[...]) * (gate * (1.0 + node_pre * (1.0 - gate)))
    ndpre = ndpre.astype(BF)
    ndpre_ref[...] = ndpre
    gathered_grad = dot_t(ndpre, win_ref[width:])
    gg_ref[...] = gathered_grad
    back = start_copies([(ndpre_ref, ndpre_out), (gg_ref, gg_out)], sems, done)
    high, low = split2(gathered_grad)
    for ref, part in ((high_ref, high), (low_ref, low)):
        ref[...] = jnp.zeros_like(ref)
        ref[own] = part

    def backward(i, carry):
        rows = pl.ds(pl.multiple_of(i * TILE, TILE), TILE)
        hot = hot_rows(ids_ref[1:2, rows], 0, slots)
        upstream = dot(hot, high_ref[...]) + dot(hot, low_ref[...])
        dsum = norm_back(upstream, normed_ref[rows, :], scale_ref[rows, :1], egain_ref[...])
        dpre_ref[rows, :] = (dot_t(dsum.astype(BF), wo_ref[...]) * pre_ref[rows, :]).astype(BF)
        return carry

    lax.fori_loop(0, steps, backward, 0)

    back += start_copies([(dpre_ref, dpre_out)], sems, done + 2)
    dpre = dpre_ref[...]
    hub_sums_ref[...] = dot(hot_cols(ids_ref[0:1, :], slots, hub_count), dpre).astype(BF)
    back += start_copies([(hub_sums_ref, hub_sums_out)], sems, done + 3)
    gathered_ref[...] = dot(hot_cols(ids_ref[0:1, :], 0, slots), dpre)
    back += start_copies([(gathered_ref.at[pl.ds(RIM, node_count)], own_out)], sems, done + 4)
    start = pl.multiple_of(core_ref[0] * (RIM + node_count), 16)
    rim_ref[...] = gathered_ref[pl.ds(start, RIM), :].astype(BF)
    for copy in back:
        copy.wait()


def late_kernel(
    core_ref, dpre_in, ids_ref, gg_in, ndpre_in, own_in, cot_in, we_in, ws_in, wr_in, win_in,
    egrad_ref, base_ref, flag_ref,
    dpre_ref, gg_ref, ndpre_ref, own_ref, cot_ref, we_ref, ws_ref, wr_ref, win_ref,
    high_ref, low_ref, sems,
):
    node_count, width = cot_in.shape
    slots = 2 * RIM + node_count
    own = slice(RIM, RIM + node_count)
    half = egrad_ref.shape[0]
    copies = start_copies(
        [
            (gg_in, gg_ref),
            (dpre_in, dpre_ref),
            (we_in, we_ref),
            (ndpre_in, ndpre_ref),
            (own_in, own_ref),
            (cot_in, cot_ref),
            (win_in.at[pl.ds(0, width)], win_ref),
            (ws_in, ws_ref),
            (wr_in, wr_ref),
        ],
        sems,
    )
    for copy in copies:
        copy.wait()
    high, low = split2(gg_ref[...])
    for ref, part in ((high_ref, high), (low_ref, low)):
        ref[...] = jnp.zeros_like(ref)
        ref[own] = part
    rows = pl.ds(pl.multiple_of(core_ref[0] * half, half), half)
    hot = hot_rows(ids_ref[1:2, rows], 0, slots)
    upstream = dot(hot, high_ref[...]) + dot(hot, low_ref[...])
    egrad_ref[...] = (upstream + dot_t(dpre_ref[rows, :], we_ref[...])).astype(BF)
    base = cot_ref[...].astype(F32) + dot_t(ndpre_ref[...], win_ref[...])
    recv = dot(hot_cols(ids_ref[1:2, :], RIM, node_count), dpre_ref[...])
    for sums, weight in ((own_ref[...], ws_ref), (recv, wr_ref)):
        high, low = split2(sums)
        base += dot_t(high, weight[...]) + dot_t(low, weight[...])
    base_ref[...] = base
    flag_ref[...] = jnp.zeros_like(flag_ref)


def last_kernel(hub_ref, rims_in, base_in, ws_in, out_ref, rims_ref, base_ref, ws_ref, sums_ref, sems):
    node_count = base_in.shape[0]
    copies = start_copies([(rims_in, rims_ref), (ws_in, ws_ref), (base_in, base_ref)], sems)
    hub = hub_ref[0]
    for z in range(1, hub_ref.shape[0]):
        hub += hub_ref[z]
    rows = [
        jnp.concatenate([hub[4 * r + j : 4 * r + j + 1] for j in range(4)], axis=1)
        for r in range(HUB_DEV)
    ]
    sums_ref[...] = jnp.zeros_like(sums_ref)
    copies[0].wait()
    sums_ref[:RIM] = rims_ref[RIM:].astype(F32)
    for r in range(HUB_DEV):
        sums_ref[r : r + 1] += rows[r]
    sums_ref[node_count - RIM :] += rims_ref[:RIM].astype(F32)
    high, low = split2(sums_ref[...])
    copies[1].wait()
    extra = dot_t(high, ws_ref[...]) + dot_t(low, ws_ref[...])
    copies[2].wait()
    out_ref[...] = (base_ref[...] + extra).astype(BF)


def both_ways(x, step):
    count = math.prod(lax.axis_size(a) for a in SPACE)
    pairs = [
        (2 * i + c, 2 * (i + d) + c)
        for i in range(count)
        for c, d in ((0, step), (1, -step))
        if 0 <= i + d < count
    ]
    return lax.ppermute(x, ALL, pairs)


def body(
    nodes,
    edges,
    senders,
    receivers,
    edge_proj,
    send_proj,
    recv_proj,
    edge_bias,
    edge_out,
    edge_gain,
    edge_shift,
    node_in,
    node_bias,
    node_out,
    node_gain,
    node_shift,
    node_cot,
):
    node_count, width = nodes.shape
    half = edges.shape[0]
    edge_count = 2 * half
    steps = edge_count // TILE
    ny, nz, nx = (lax.axis_size(a) for a in SPACE)
    plane = ny * nx
    hub_count = plane * HUB_DEV * nz
    slots = 2 * RIM + node_count
    core = lax.axis_index("c").astype(I32)
    own_block = lax.axis_index(SPACE)
    row = lambda v: (v.reshape(1, width), VM)
    wide = lambda rows, kind=BF: pltpu.VMEM((rows, width), kind)
    square = 2 * width * width

    my_hub, my_rim = call(
        prep_kernel,
        [(core.reshape(1), SM), (nodes, HB)],
        [((nz, 8, LANES), F32, VM), ((RIM, width), BF, VM)],
        [wide(16)],
        copies=2,
        name="prep",
    )
    by_z = lax.all_to_all(my_hub, "z", 0, 0)
    rim = both_ways(my_rim, 1)
    (spread,) = call(
        spread_kernel,
        [(by_z.reshape(nz * 8, LANES), VM)],
        [((plane, HUB_DEV * nz, width), BF, VM)],
        room=54000,
        name="spread",
    )
    hubs = lax.all_to_all(spread, PLANE, 0, 0).reshape(hub_count, width)

    rims = lax.all_gather(rim, "c", axis=0, tiled=True)
    all_edges = lax.all_gather(edges, "c", axis=0, tiled=True)
    ids = lax.all_gather(jnp.stack([senders, receivers]), "c", axis=1, tiled=True)
    block = ids[0] // node_count
    line = ids[0] - block * node_count
    hub_y, hub_zx = block // (nz * nx), block % (nz * nx)
    hub_z, hub_x = hub_zx // nx, hub_zx % nx
    hub_slot = ((hub_y * nx + hub_x) * HUB_DEV + line) * nz + hub_z
    slot = jnp.where(
        block == own_block,
        RIM + line,
        jnp.where(
            (block == own_block - 1) & (line >= node_count - RIM),
            line - (node_count - RIM),
            jnp.where(
                (block == own_block + 1) & (line < RIM),
                RIM + node_count + line,
                slots + hub_slot,
            ),
        ),
    )
    ids = jnp.stack([slot, ids[1] - own_block * node_count + RIM])

    (near,) = call(
        near_kernel,
        [
            (all_edges, HB), (ids, VM), (nodes, HB), (rims, HB),
            (edge_proj, HB), (send_proj, HB), (recv_proj, HB), row(edge_bias),
        ],
        [((edge_count, width), F32, HB)],
        [wide(edge_count)] + [wide(slots)] + [wide(width)] * 3 + [wide(slots)] * 2
        + [wide(edge_count, F32)],
        copies=7 + steps,
        flops=square * (edge_count * 2 + 2 * slots),
        name="near",
    )
    new_nodes, dpre, hub_sums, my_rim, own_sums, gathered_grad, node_dpre = call(
        main_kernel,
        [
            (core.reshape(1), SM), (hubs, HB), (near, HB), (all_edges, HB), (ids, VM), (nodes, HB),
            (node_cot, HB), (send_proj, HB), (edge_out, HB), (node_in, HB), (node_out, HB),
            row(edge_gain), row(edge_shift), row(node_bias), row(node_gain), row(node_shift),
        ],
        [
            ((node_count, width), BF, VM),
            ((edge_count, width), BF, HB),
            ((hub_count, width), BF, HB),
            ((RIM, width), BF, VM),
            ((node_count, width), F32, HB),
            ((node_count, width), F32, HB),
            ((node_count, width), BF, HB),
        ],
        [wide(hub_count), wide(edge_count, F32), wide(edge_count)]
        + [wide(node_count)] * 2 + [wide(width)] * 2 + [wide(2 * width), wide(width)]
        + [wide(edge_count), wide(hub_count), wide(node_count, F32), wide(node_count)]
        + [wide(hub_count), wide(edge_count, F32), pltpu.VMEM((edge_count, LANES), F32)]
        + [wide(slots, F32), wide(slots), wide(slots)],
        copies=12 + 2 * steps,
        flops=square * (edge_count * 6 + hub_count),
        room=0,
        name="main",
    )

    hub_back = lax.all_to_all(hub_sums.reshape(plane, HUB_DEV * nz, width), PLANE, 0, 0)
    rim = both_ways(my_rim, -1)
    edge_grad, base, flag = call(
        late_kernel,
        [
            (core.reshape(1), SM), (dpre, HB), (ids, VM), (gathered_grad, HB), (node_dpre, HB),
            (own_sums, HB), (node_cot, HB), (edge_proj, HB), (send_proj, HB), (recv_proj, HB),
            (node_in, HB),
        ],
        [((half, width), BF, VM), ((node_count, width), F32, VM), ((8, LANES), F32, VM)],
        [wide(edge_count), wide(node_count, F32), wide(node_count), wide(node_count, F32)]
        + [wide(node_count)] + [wide(width)] * 4 + [wide(slots)] * 2,
        copies=9,
        flops=square * edge_count * 2,
        name="late",
    )
    by_z, rim = call(
        gather_kernel,
        [(hub_back, HB), (rim, HB), (flag, HB)],
        [((nz * 8, LANES), F32, VM), ((RIM, width), BF, VM)],
        [pltpu.VMEM((plane, HUB_DEV * nz, width), BF)],
        copies=5,
        room=54000,
        name="gather",
    )
    hub_back = lax.all_to_all(by_z.reshape(nz, 8, LANES), "z", 0, 0)
    rims = lax.all_gather(rim, "c", axis=0, tiled=True)
    (node_grad,) = call(
        last_kernel,
        [(hub_back, VM), (rims, HB), (base, HB), (send_proj, HB)],
        [((node_count, width), BF, VM)],
        [wide(2 * RIM), wide(node_count, F32), wide(width), wide(node_count, F32)],
        copies=3,
        flops=square * node_count * 2,
        room=0,
        name="last",
    )
    return new_nodes, node_grad, edge_grad


def solution(mesh):
    fine = Mesh(np.asarray(mesh.devices).reshape(*SHAPE, 2), ALL)
    rows, both = P(SPACE, None), P(ALL, None)
    whole = P()
    in_specs = (rows, both, P(ALL), P(ALL)) + (whole,) * 12 + (rows,)
    return jax.shard_map(
        body, mesh=fine, in_specs=in_specs, out_specs=(rows, rows, both), check_vma=False
    )
```

```python
import functools
import math

import jax
import jax.numpy as jnp
import numpy as np
from jax import lax
from jax.experimental import pallas as pl
from jax.experimental.pallas import tpu as pltpu
from jax.sharding import Mesh, PartitionSpec as P

RIM = 48
HUB_DEV = 2
EPS = 1e-05
BF = jnp.bfloat16
F32 = jnp.float32
I32 = jnp.int32
ALL = ("y", "z", "x", "c")
SPACE = ("y", "z", "x")
LANES = 128
TILE = 256
SHAPE = (4, 16, 4)
GRANT = 60 * 1024 * 1024


def dot(a, b):
    return jnp.dot(a, b, preferred_element_type=F32)


def dot_t(a, b):
    return lax.dot_general(a, b, (((1,), (1,)), ((), ())), preferred_element_type=F32)


def split2(v):
    high = v.astype(BF)
    return high, (v - high.astype(F32)).astype(BF)


def row_mean(v):
    return jnp.mean(v, axis=-1, keepdims=True)


def layer_stats(values):
    centred = values - row_mean(values)
    inv_scale = lax.rsqrt(row_mean(centred * centred) + EPS)
    return centred * inv_scale, inv_scale


def norm_back(upstream, normed, inv_scale, gain_vec):
    scaled = upstream * gain_vec
    return inv_scale * (scaled - row_mean(scaled) - normed * row_mean(scaled * normed))


def hot_rows(ids, first, count):
    edges = ids.shape[1]
    column = jnp.broadcast_to(ids - first, (LANES, edges)).T
    lane = lax.broadcasted_iota(I32, (edges, LANES), 1)
    parts = [
        jnp.where(column == lane + k, 1.0, 0.0).astype(BF) for k in range(0, count, LANES)
    ]
    return jnp.concatenate(parts, axis=1)[:, :count]


def hot_cols(ids, first, count):
    edges = ids.shape[1]
    slot = lax.broadcasted_iota(I32, (count, edges), 0)
    return jnp.where(slot == ids - first, 1.0, 0.0).astype(BF)


VM = pl.BlockSpec(memory_space=pltpu.VMEM)
SM = pl.BlockSpec(memory_space=pltpu.SMEM)
HB = pl.BlockSpec(memory_space=pltpu.HBM)


def call(kernel, ins, outs, scratch=(), copies=0, flops=0, room=0, name=None):
    shapes = [jax.ShapeDtypeStruct(s, d) for s, d, _ in outs]
    args = [a for a, _ in ins]
    moved = sum(math.prod(o.shape) * o.dtype.itemsize for o in shapes + args)
    scratch = list(scratch)
    if copies:
        scratch.append(pltpu.SemaphoreType.DMA((copies,)))
    return pl.pallas_call(
        kernel,
        out_shape=shapes,
        in_specs=[spec for _, spec in ins],
        out_specs=[spec for _, _, spec in outs],
        scratch_shapes=scratch,
        compiler_params=pltpu.CompilerParams(vmem_limit_bytes=GRANT - room * 1024),
        cost_estimate=pl.CostEstimate(flops=flops, bytes_accessed=moved, transcendentals=0),
        name=name,
    )(*args)


def start_copies(pairs, sems, first=0):
    copies = [
        pltpu.make_async_copy(src, dst, sems.at[first + k]) for k, (src, dst) in enumerate(pairs)
    ]
    for copy in copies:
        copy.start()
    return copies


def prep_kernel(core_ref, nodes_ref, hub_ref, rim_ref, head_ref, sems):
    node_count = nodes_ref.shape[0]
    start = pl.multiple_of((1 - core_ref[0]) * (node_count - RIM), 16)
    head, rim = start_copies(
        [(nodes_ref.at[:16], head_ref), (nodes_ref.at[pl.ds(start, RIM)], rim_ref)], sems
    )
    head.wait()
    rows = head_ref[...].astype(F32)
    tile = jnp.concatenate(
        [rows[r : r + 1, j * LANES : (j + 1) * LANES] for r in range(HUB_DEV) for j in range(4)],
        axis=0,
    ).astype(BF)
    for b in range(hub_ref.shape[0]):
        hub_ref[b] = tile
    rim.wait()


def near_kernel(
    edges_in, ids_ref, nodes_in, rims_in, we_in, ws_in, wr_in, bias_ref,
    pre_out,
    edges_ref, frame_ref, we_ref, ws_ref, wr_ref, send_ref, recv_ref, pre_ref, sems,
):
    node_count = nodes_in.shape[0]
    slots = 2 * RIM + node_count
    tiles = [pl.ds(i * TILE, TILE) for i in range(edges_in.shape[0] // TILE)]
    copies = start_copies(
        [
            (nodes_in, frame_ref.at[pl.ds(RIM, node_count)]),
            (rims_in.at[pl.ds(0, RIM)], frame_ref.at[pl.ds(0, RIM)]),
            (rims_in.at[pl.ds(RIM, RIM)], frame_ref.at[pl.ds(RIM + node_count, RIM)]),
            (ws_in, ws_ref),
            (wr_in, wr_ref),
            (we_in, we_ref),
        ]
        + [(edges_in.at[rows], edges_ref.at[rows]) for rows in tiles],
        sems,
    )
    for copy in copies[:4]:
        copy.wait()
    send_ref[...] = dot(frame_ref[...], ws_ref[...]).astype(BF)
    copies[4].wait()
    recv_ref[...] = dot(frame_ref[...], wr_ref[...]).astype(BF)
    copies[5].wait()
    back = []
    for i, rows in enumerate(tiles):
        copies[6 + i].wait()
        pre = dot(edges_ref[rows, :], we_ref[...])
        pre += dot(hot_rows(ids_ref[0:1, rows], 0, slots), send_ref[...])
        pre += dot(hot_rows(ids_ref[1:2, rows], 0, slots), recv_ref[...])
        pre_ref[rows, :] = pre + bias_ref[...]
        back += start_copies([(pre_ref.at[rows], pre_out.at[rows])], sems, len(copies) + i)
    for copy in back:
        copy.wait()


def main_kernel(
    core_ref, hubs_in, pre_in, edges_in, ids_ref, nodes_in, cot_in, ws_in, wo_in, win_in, wout_in,
    egain_ref, eshift_ref, nbias_ref, ngain_ref, nshift_ref,
    new_ref, dpre_out, hub_sums_out, rim_ref, own_out, gg_out, ndpre_out,
    hubs_ref, pre_ref, edges_ref, nodes_ref, cot_ref, ws_ref, wo_ref, win_ref, wout_ref,
    dpre_ref, hub_sums_ref, gg_ref, ndpre_ref,
    wide_ref, rows_ref, terms_ref, normed_ref, scale_ref, gathered_ref, high_ref, low_ref, sems,
):
    node_count, width = nodes_in.shape
    blocks = hubs_in.shape[0] // 8
    hub_count = HUB_DEV * blocks
    edge_count = edges_in.shape[0]
    steps = edge_count // TILE
    slots = 2 * RIM + node_count
    own = slice(RIM, RIM + node_count)
    tiles = [pl.ds(i * TILE, TILE) for i in range(steps)]
    hubs, ws, wo, nodes, cot, win, wout, *rest = start_copies(
        [
            (hubs_in, hubs_ref),
            (ws_in, ws_ref),
            (wo_in, wo_ref),
            (nodes_in, nodes_ref),
            (cot_in, cot_ref),
            (win_in, win_ref),
            (wout_in, wout_ref),
        ]
        + [(pre_in.at[rows], pre_ref.at[rows]) for rows in tiles]
        + [(edges_in.at[rows], edges_ref.at[rows]) for rows in tiles],
        sems,
    )
    done = 7 + 2 * steps
    gathered_ref[...] = jnp.zeros_like(gathered_ref)
    spots = [
        (
            pl.ds(4 * r + j, blocks, stride=8),
            slice(r * blocks, (r + 1) * blocks),
            slice(j * LANES, (j + 1) * LANES),
        )
        for r in range(HUB_DEV)
        for j in range(4)
    ]
    hubs.wait()
    wide_ref[...] = hubs_ref[...].astype(F32)
    for spot, line, lane in spots:
        rows_ref[line, lane] = wide_ref[spot, :].astype(BF)
    ws.wait()
    terms_ref[...] = dot(rows_ref[...], ws_ref[...]).astype(BF)
    wo.wait()
    for i, rows in enumerate(tiles):
        rest[i].wait()
        rest[steps + i].wait()
        pre = pre_ref[rows, :] + dot(hot_rows(ids_ref[0:1, rows], slots, hub_count), terms_ref[...])
        gate = jax.nn.sigmoid(pre)
        pre_ref[rows, :] = gate * (1.0 + pre * (1.0 - gate))
        edge_sum = dot((pre * gate).astype(BF), wo_ref[...])
        normed, scale = layer_stats(edge_sum)
        normed_ref[rows, :] = normed
        scale_ref[rows, :] = jnp.broadcast_to(scale, (TILE, LANES))
        new_edges = edges_ref[rows, :].astype(F32) + normed * egain_ref[...] + eshift_ref[...]
        gathered_ref[...] += dot(hot_cols(ids_ref[1:2, rows], 0, slots), new_edges.astype(BF))

    for copy in (nodes, cot, win, wout):
        copy.wait()
    nodes = nodes_ref[...]
    gathered = gathered_ref[own].astype(BF)
    node_pre = dot(nodes, win_ref[:width]) + dot(gathered, win_ref[width:]) + nbias_ref[...]
    gate = jax.nn.sigmoid(node_pre)
    node_mix = dot((node_pre * gate).astype(BF), wout_ref[...])
    normed, scale = layer_stats(node_mix)
    new_nodes = nodes.astype(F32) + normed * ngain_ref[...] + nshift_ref[...]
    new_ref[...] = new_nodes.astype(BF)
    dmix = norm_back(cot_ref[...].astype(F32), normed, scale, ngain_ref[...]).astype(BF)
    ndpre = dot_t(dmix, wout_ref[...]) * (gate * (1.0 + node_pre * (1.0 - gate)))
    ndpre = ndpre.astype(BF)
    ndpre_ref[...] = ndpre
    gathered_grad = dot_t(ndpre, win_ref[width:])
    gg_ref[...] = gathered_grad
    back = start_copies([(ndpre_ref, ndpre_out), (gg_ref, gg_out)], sems, done)
    high, low = split2(gathered_grad)
    for ref, part in ((high_ref, high), (low_ref, low)):
        ref[...] = jnp.zeros_like(ref)
        ref[own] = part

    for rows in tiles:
        hot = hot_rows(ids_ref[1:2, rows], 0, slots)
        upstream = dot(hot, high_ref[...]) + dot(hot, low_ref[...])
        dsum = norm_back(upstream, normed_ref[rows, :], scale_ref[rows, :1], egain_ref[...])
        dpre_ref[rows, :] = (dot_t(dsum.astype(BF), wo_ref[...]) * pre_ref[rows, :]).astype(BF)

    back += start_copies([(dpre_ref, dpre_out)], sems, done + 2)
    dpre = dpre_ref[...]
    hub_sums = dot(hot_cols(ids_ref[0:1, :], slots, hub_count), dpre)
    for spot, line, lane in spots:
        wide_ref[spot, :] = hub_sums[line, lane]
    hub_sums_ref[...] = wide_ref[...].astype(BF)
    back += start_copies([(hub_sums_ref, hub_sums_out)], sems, done + 3)
    gathered_ref[...] = dot(hot_cols(ids_ref[0:1, :], 0, slots), dpre)
    back += start_copies([(gathered_ref.at[pl.ds(RIM, node_count)], own_out)], sems, done + 4)
    start = pl.multiple_of(core_ref[0] * (RIM + node_count), 16)
    rim_ref[...] = gathered_ref[pl.ds(start, RIM), :].astype(BF)
    for copy in back:
        copy.wait()


def late_kernel(
    core_ref, dpre_in, ids_ref, gg_in, ndpre_in, own_in, cot_in, we_in, ws_in, wr_in, win_in,
    egrad_ref, base_ref,
    dpre_ref, gg_ref, ndpre_ref, own_ref, cot_ref, we_ref, ws_ref, wr_ref, win_ref,
    high_ref, low_ref, sems,
):
    node_count, width = cot_in.shape
    slots = 2 * RIM + node_count
    own = slice(RIM, RIM + node_count)
    half = egrad_ref.shape[0]
    copies = start_copies(
        [
            (gg_in, gg_ref),
            (dpre_in, dpre_ref),
            (we_in, we_ref),
            (ndpre_in, ndpre_ref),
            (own_in, own_ref),
            (cot_in, cot_ref),
            (win_in.at[pl.ds(0, width)], win_ref),
            (ws_in, ws_ref),
            (wr_in, wr_ref),
        ],
        sems,
    )
    for copy in copies:
        copy.wait()
    high, low = split2(gg_ref[...])
    for ref, part in ((high_ref, high), (low_ref, low)):
        ref[...] = jnp.zeros_like(ref)
        ref[own] = part
    rows = pl.ds(pl.multiple_of(core_ref[0] * half, half), half)
    hot = hot_rows(ids_ref[1:2, rows], 0, slots)
    upstream = dot(hot, high_ref[...]) + dot(hot, low_ref[...])
    egrad_ref[...] = (upstream + dot_t(dpre_ref[rows, :], we_ref[...])).astype(BF)
    base = cot_ref[...].astype(F32) + dot_t(ndpre_ref[...], win_ref[...])
    recv = dot(hot_cols(ids_ref[1:2, :], RIM, node_count), dpre_ref[...])
    for sums, weight in ((own_ref[...], ws_ref), (recv, wr_ref)):
        high, low = split2(sums)
        base += dot_t(high, weight[...]) + dot_t(low, weight[...])
    base_ref[...] = base


def last_kernel(
    hub_in, rims_in, base_in, ws_in, out_ref, hub_ref, rims_ref, base_ref, ws_ref, sums_ref, sems
):
    node_count = base_in.shape[0]
    copies = start_copies(
        [(hub_in, hub_ref), (rims_in, rims_ref), (ws_in, ws_ref), (base_in, base_ref)], sems
    )
    blocks = hub_ref.shape[0] // 8
    sums_ref[...] = jnp.zeros_like(sums_ref)
    copies[0].wait()
    hub = hub_ref[...].astype(F32).reshape(blocks, 8, LANES).sum(0)
    rows = [
        jnp.concatenate([hub[4 * r + j : 4 * r + j + 1] for j in range(4)], axis=1)
        for r in range(HUB_DEV)
    ]
    copies[1].wait()
    sums_ref[:RIM] = rims_ref[RIM:].astype(F32)
    for r in range(HUB_DEV):
        sums_ref[r : r + 1] += rows[r]
    sums_ref[node_count - RIM :] += rims_ref[:RIM].astype(F32)
    high, low = split2(sums_ref[...])
    copies[2].wait()
    extra = dot_t(high, ws_ref[...]) + dot_t(low, ws_ref[...])
    copies[3].wait()
    out_ref[...] = (base_ref[...] + extra).astype(BF)


def both_ways(x, step):
    count = math.prod(lax.axis_size(a) for a in SPACE)
    pairs = [
        (2 * i + c, 2 * (i + d) + c)
        for i in range(count)
        for c, d in ((0, step), (1, -step))
        if 0 <= i + d < count
    ]
    return lax.ppermute(x, ALL, pairs)


def body(
    nodes,
    edges,
    senders,
    receivers,
    edge_proj,
    send_proj,
    recv_proj,
    edge_bias,
    edge_out,
    edge_gain,
    edge_shift,
    node_in,
    node_bias,
    node_out,
    node_gain,
    node_shift,
    node_cot,
):
    node_count, width = nodes.shape
    half = edges.shape[0]
    edge_count = 2 * half
    steps = edge_count // TILE
    blocks = math.prod(lax.axis_size(a) for a in SPACE)
    hub_count = HUB_DEV * blocks
    slots = 2 * RIM + node_count
    core = lax.axis_index("c").astype(I32)
    own_block = lax.axis_index(SPACE)
    row = lambda v: (v.reshape(1, width), VM)
    wide = lambda rows, kind=BF: pltpu.VMEM((rows, width), kind)
    square = 2 * width * width

    my_hub, my_rim = call(
        prep_kernel,
        [(core.reshape(1), SM), (nodes, HB)],
        [((blocks, 8, LANES), BF, VM), ((RIM, width), BF, VM)],
        [wide(16)],
        copies=2,
        name="prep",
    )
    hubs = lax.all_to_all(my_hub, SPACE, 0, 0).reshape(blocks * 8, LANES)
    rim = both_ways(my_rim, 1)

    rims = lax.all_gather(rim, "c", axis=0, tiled=True)
    all_edges = lax.all_gather(edges, "c", axis=0, tiled=True)
    ids = lax.all_gather(jnp.stack([senders, receivers]), "c", axis=1, tiled=True)
    block = ids[0] // node_count
    line = ids[0] - block * node_count
    slot = jnp.where(
        block == own_block,
        RIM + line,
        jnp.where(
            (block == own_block - 1) & (line >= node_count - RIM),
            line - (node_count - RIM),
            jnp.where(
                (block == own_block + 1) & (line < RIM),
                RIM + node_count + line,
                slots + line * blocks + block,
            ),
        ),
    )
    ids = jnp.stack([slot, ids[1] - own_block * node_count + RIM])

    (near,) = call(
        near_kernel,
        [
            (all_edges, HB), (ids, VM), (nodes, HB), (rims, HB),
            (edge_proj, HB), (send_proj, HB), (recv_proj, HB), row(edge_bias),
        ],
        [((edge_count, width), F32, HB)],
        [wide(edge_count)] + [wide(slots)] + [wide(width)] * 3 + [wide(slots)] * 2
        + [wide(edge_count, F32)],
        copies=6 + 2 * steps,
        flops=square * (edge_count * 2 + 2 * slots),
        name="near",
    )
    new_nodes, dpre, hub_sums, my_rim, own_sums, gathered_grad, node_dpre = call(
        main_kernel,
        [
            (core.reshape(1), SM), (hubs, HB), (near, HB), (all_edges, HB), (ids, VM), (nodes, HB),
            (node_cot, HB), (send_proj, HB), (edge_out, HB), (node_in, HB), (node_out, HB),
            row(edge_gain), row(edge_shift), row(node_bias), row(node_gain), row(node_shift),
        ],
        [
            ((node_count, width), BF, VM),
            ((edge_count, width), BF, HB),
            ((blocks * 8, LANES), BF, HB),
            ((RIM, width), BF, VM),
            ((node_count, width), F32, HB),
            ((node_count, width), F32, HB),
            ((node_count, width), BF, HB),
        ],
        [pltpu.VMEM((blocks * 8, LANES), BF), wide(edge_count, F32), wide(edge_count)]
        + [wide(node_count)] * 2 + [wide(width)] * 2 + [wide(2 * width), wide(width)]
        + [wide(edge_count), pltpu.VMEM((blocks * 8, LANES), BF), wide(node_count, F32)]
        + [wide(node_count), pltpu.VMEM((blocks * 8, LANES), F32), wide(hub_count)]
        + [wide(hub_count), wide(edge_count, F32), pltpu.VMEM((edge_count, LANES), F32)]
        + [wide(slots, F32), wide(slots), wide(slots)],
        copies=12 + 2 * steps,
        flops=square * (edge_count * 6 + hub_count),
        room=0,
        name="main",
    )

    hub_back = lax.all_to_all(hub_sums.reshape(blocks, 8, LANES), SPACE, 0, 0)
    hub_back = hub_back.reshape(blocks * 8, LANES)
    rim = both_ways(my_rim, -1)
    edge_grad, base = call(
        late_kernel,
        [
            (core.reshape(1), SM), (dpre, HB), (ids, VM), (gathered_grad, HB), (node_dpre, HB),
            (own_sums, HB), (node_cot, HB), (edge_proj, HB), (send_proj, HB), (recv_proj, HB),
            (node_in, HB),
        ],
        [((half, width), BF, VM), ((node_count, width), F32, VM)],
        [wide(edge_count), wide(node_count, F32), wide(node_count), wide(node_count, F32)]
        + [wide(node_count)] + [wide(width)] * 4 + [wide(slots)] * 2,
        copies=9,
        flops=square * edge_count * 2,
        name="late",
    )
    rims = lax.all_gather(rim, "c", axis=0, tiled=True)
    (node_grad,) = call(
        last_kernel,
        [(hub_back, HB), (rims, HB), (base, HB), (send_proj, HB)],
        [((node_count, width), BF, VM)],
        [pltpu.VMEM((blocks * 8, LANES), BF), wide(2 * RIM), wide(node_count, F32), wide(width)]
        + [wide(node_count, F32)],
        copies=4,
        flops=square * node_count * 2,
        room=0,
        name="last",
    )
    return new_nodes, node_grad, edge_grad


def solution(mesh):
    fine = Mesh(np.asarray(mesh.devices).reshape(*SHAPE, 2), ALL)
    rows, both = P(SPACE, None), P(ALL, None)
    whole = P()
    in_specs = (rows, both, P(ALL), P(ALL)) + (whole,) * 12 + (rows,)
    return jax.shard_map(
        body, mesh=fine, in_specs=in_specs, out_specs=(rows, rows, both), check_vma=False
    )
```

```python
import math

import jax
import jax.numpy as jnp
import numpy as np
from jax import lax
from jax.experimental import pallas as pl
from jax.experimental.pallas import tpu as pltpu
from jax.sharding import Mesh, PartitionSpec as P

RIM = 48
HUB_DEV = 2
EPS = 1e-05
BF = jnp.bfloat16
F32 = jnp.float32
I32 = jnp.int32
ALL = ("y", "z", "x", "c")
SPACE = ("y", "z", "x")
PLANE = ("y", "x")
LANES = 128
TILE = 256
SHAPE = (4, 16, 4)
GRANT = 60 * 1024 * 1024


def dot(a, b):
    return jnp.dot(a, b, preferred_element_type=F32)


def dot_t(a, b):
    return lax.dot_general(a, b, (((1,), (1,)), ((), ())), preferred_element_type=F32)


def split2(v):
    high = v.astype(BF)
    return high, (v - high.astype(F32)).astype(BF)


def times(sums, weight_ref):
    high, low = split2(sums)
    return (dot_t(high, weight_ref[...]) + dot_t(low, weight_ref[...])).astype(BF)


def row_mean(v):
    return jnp.mean(v, axis=-1, keepdims=True)


def layer_stats(values):
    centred = values - row_mean(values)
    inv_scale = lax.rsqrt(row_mean(centred * centred) + EPS)
    return centred * inv_scale, inv_scale


def norm_back(upstream, normed, inv_scale, gain_vec):
    scaled = upstream * gain_vec
    return inv_scale * (scaled - row_mean(scaled) - normed * row_mean(scaled * normed))


def hot_rows(ids, first, count):
    edges = ids.shape[1]
    column = jnp.broadcast_to(ids - first, (LANES, edges)).T
    lane = lax.broadcasted_iota(I32, (edges, LANES), 1)
    parts = [
        jnp.where(column == lane + k, 1.0, 0.0).astype(BF) for k in range(0, count, LANES)
    ]
    return jnp.concatenate(parts, axis=1)[:, :count]


def hot_cols(ids, first, count):
    edges = ids.shape[1]
    slot = lax.broadcasted_iota(I32, (count, edges), 0)
    return jnp.where(slot == ids - first, 1.0, 0.0).astype(BF)


VM = pl.BlockSpec(memory_space=pltpu.VMEM)
SM = pl.BlockSpec(memory_space=pltpu.SMEM)
HB = pl.BlockSpec(memory_space=pltpu.HBM)


def call(kernel, ins, outs, scratch=(), copies=0, flops=0, room=0):
    shapes = [jax.ShapeDtypeStruct(s, d) for s, d, _ in outs]
    args = [a for a, _ in ins]
    moved = sum(math.prod(o.shape) * o.dtype.itemsize for o in shapes + args)
    scratch = list(scratch)
    if copies:
        scratch.append(pltpu.SemaphoreType.DMA((copies,)))
    return pl.pallas_call(
        kernel,
        out_shape=shapes,
        in_specs=[spec for _, spec in ins],
        out_specs=[spec for _, _, spec in outs],
        scratch_shapes=scratch,
        compiler_params=pltpu.CompilerParams(vmem_limit_bytes=GRANT - room * 1024),
        cost_estimate=pl.CostEstimate(flops=flops, bytes_accessed=moved, transcendentals=0),
    )(*args)


def edge_pairs(core_ref, own_in, other_in, edges_ref):
    half = own_in.shape[0]
    return [
        (src, edges_ref.at[pl.ds(pl.multiple_of(at * half, half), half)])
        for src, at in ((own_in, core_ref[0]), (other_in, 1 - core_ref[0]))
    ]


def start_copies(pairs, sems, first=0):
    copies = [
        pltpu.make_async_copy(src, dst, sems.at[first + k]) for k, (src, dst) in enumerate(pairs)
    ]
    for copy in copies:
        copy.start()
    return copies


def prep_kernel(core_ref, nodes_ref, hub_ref, rim_ref, head_ref, sems):
    node_count = nodes_ref.shape[0]
    start = pl.multiple_of((1 - core_ref[0]) * (node_count - RIM), 16)
    head, rim = start_copies(
        [(nodes_ref.at[:16], head_ref), (nodes_ref.at[pl.ds(start, RIM)], rim_ref)], sems
    )
    head.wait()
    rows = head_ref[...].astype(F32)
    tile = jnp.concatenate(
        [rows[r : r + 1, j * LANES : (j + 1) * LANES] for r in range(HUB_DEV) for j in range(4)],
        axis=0,
    )
    for z in range(hub_ref.shape[0]):
        hub_ref[z] = tile
    rim.wait()


def spread_kernel(rows_ref, out_ref):
    nz = rows_ref.shape[0] // 8
    parts = []
    for r in range(HUB_DEV):
        lanes = [rows_ref[pl.ds(4 * r + j, nz, stride=8), :] for j in range(4)]
        parts.append(jnp.concatenate(lanes, axis=1))
    rows = jnp.concatenate(parts, axis=0).astype(BF)
    for p in range(out_ref.shape[0]):
        out_ref[p] = rows


def gather_kernel(sums_ref, out_ref, buf_ref, sems):
    planes = sums_ref.shape[0]
    nz = out_ref.shape[0] // 8
    quarter = planes // 4
    pairs = [
        (sums_ref.at[pl.ds(k * quarter, quarter)], buf_ref.at[pl.ds(k * quarter, quarter)])
        for k in range(4)
    ]
    copies = start_copies(pairs, sems)
    total = jnp.zeros(buf_ref.shape[1:], F32)
    for p in range(planes):
        if p % quarter == 0:
            copies[p // quarter].wait()
        total += buf_ref[p].astype(F32)
    for r in range(HUB_DEV):
        for j in range(4):
            out_ref[pl.ds(4 * r + j, nz, stride=8), :] = total[
                r * nz : (r + 1) * nz, j * LANES : (j + 1) * LANES
            ]


def near_kernel(
    core_ref, own_in, other_in, ids_ref, nodes_in, rims_in, we_in, ws_in, wr_in, bias_ref,
    pre_out,
    edges_ref, frame_ref, we_ref, ws_ref, wr_ref, send_ref, recv_ref, pre_ref, sems,
):
    node_count = nodes_in.shape[0]
    slots = 2 * RIM + node_count
    copies = start_copies(
        [
            (nodes_in, frame_ref.at[pl.ds(RIM, node_count)]),
            (rims_in.at[pl.ds(0, RIM)], frame_ref.at[pl.ds(0, RIM)]),
            (rims_in.at[pl.ds(RIM, RIM)], frame_ref.at[pl.ds(RIM + node_count, RIM)]),
            (ws_in, ws_ref),
            (wr_in, wr_ref),
            (we_in, we_ref),
        ]
        + edge_pairs(core_ref, own_in, other_in, edges_ref),
        sems,
    )
    for copy in copies[:4]:
        copy.wait()
    send_ref[...] = dot(frame_ref[...], ws_ref[...]).astype(BF)
    copies[4].wait()
    recv_ref[...] = dot(frame_ref[...], wr_ref[...]).astype(BF)
    for copy in copies[5:]:
        copy.wait()
    back = []
    for i in range(edges_ref.shape[0] // TILE):
        rows = pl.ds(i * TILE, TILE)
        pre = dot(edges_ref[rows, :], we_ref[...])
        pre += dot(hot_rows(ids_ref[0:1, rows], 0, slots), send_ref[...])
        pre += dot(hot_rows(ids_ref[1:2, rows], 0, slots), recv_ref[...])
        pre_ref[rows, :] = pre + bias_ref[...]
        back += start_copies([(pre_ref.at[rows], pre_out.at[rows])], sems, len(copies) + i)
    for copy in back:
        copy.wait()


def main_kernel(
    core_ref, hubs_in, pre_in, own_in, other_in, ids_ref, nodes_in, cot_in, ws_in, wo_in, win_in, wout_in,
    egain_ref, eshift_ref, nbias_ref, ngain_ref, nshift_ref,
    new_ref, dpre_out, hub_sums_out, rim_ref, own_out, gg_out, ndpre_out,
    hubs_ref, pre_ref, edges_ref, nodes_ref, cot_ref, ws_ref, wo_ref, win_ref, wout_ref,
    dpre_ref, hub_sums_ref, gg_ref, ndpre_ref,
    terms_ref, normed_ref, scale_ref, gathered_ref, high_ref, low_ref, sems,
):
    node_count, width = nodes_in.shape
    hub_count = hubs_in.shape[0]
    edge_count = edges_ref.shape[0]
    steps = edge_count // TILE
    slots = 2 * RIM + node_count
    own = slice(RIM, RIM + node_count)
    tiles = [pl.ds(i * TILE, TILE) for i in range(steps)]
    hubs, ws, wo, *rest = start_copies(
        [(hubs_in, hubs_ref), (ws_in, ws_ref), (wo_in, wo_ref)]
        + [(pre_in.at[rows], pre_ref.at[rows]) for rows in tiles]
        + edge_pairs(core_ref, own_in, other_in, edges_ref)
        + [(nodes_in, nodes_ref), (cot_in, cot_ref), (win_in, win_ref), (wout_in, wout_ref)],
        sems,
    )
    done = 3 + len(rest)
    gathered_ref[...] = jnp.zeros_like(gathered_ref)
    hubs.wait()
    ws.wait()
    terms_ref[...] = dot(hubs_ref[...], ws_ref[...]).astype(BF)
    for i, rows in enumerate(tiles):
        rest[i].wait()
        if i == 0:
            wo.wait()
            rest[steps].wait()
            rest[steps + 1].wait()
        pre = pre_ref[rows, :] + dot(hot_rows(ids_ref[0:1, rows], slots, hub_count), terms_ref[...])
        gate = jax.nn.sigmoid(pre)
        pre_ref[rows, :] = gate * (1.0 + pre * (1.0 - gate))
        edge_sum = dot((pre * gate).astype(BF), wo_ref[...])
        normed, scale = layer_stats(edge_sum)
        normed_ref[rows, :] = normed
        scale_ref[rows, :] = jnp.broadcast_to(scale, (TILE, LANES))
        new_edges = edges_ref[rows, :].astype(F32) + normed * egain_ref[...] + eshift_ref[...]
        gathered_ref[...] += dot(hot_cols(ids_ref[1:2, rows], 0, slots), new_edges.astype(BF))

    for copy in rest[steps + 2 :]:
        copy.wait()
    nodes = nodes_ref[...]
    gathered = gathered_ref[own].astype(BF)
    node_pre = dot(nodes, win_ref[:width]) + dot(gathered, win_ref[width:]) + nbias_ref[...]
    gate = jax.nn.sigmoid(node_pre)
    node_mix = dot((node_pre * gate).astype(BF), wout_ref[...])
    normed, scale = layer_stats(node_mix)
    new_nodes = nodes.astype(F32) + normed * ngain_ref[...] + nshift_ref[...]
    new_ref[...] = new_nodes.astype(BF)
    dmix = norm_back(cot_ref[...].astype(F32), normed, scale, ngain_ref[...]).astype(BF)
    ndpre = dot_t(dmix, wout_ref[...]) * (gate * (1.0 + node_pre * (1.0 - gate)))
    ndpre = ndpre.astype(BF)
    ndpre_ref[...] = ndpre
    gathered_grad = dot_t(ndpre, win_ref[width:])
    gg_ref[...] = gathered_grad
    back = start_copies([(ndpre_ref, ndpre_out), (gg_ref, gg_out)], sems, done)
    high, low = split2(gathered_grad)
    for ref, part in ((high_ref, high), (low_ref, low)):
        ref[...] = jnp.zeros_like(ref)
        ref[own] = part

    for rows in tiles:
        hot = hot_rows(ids_ref[1:2, rows], 0, slots)
        upstream = dot(hot, high_ref[...]) + dot(hot, low_ref[...])
        dsum = norm_back(upstream, normed_ref[rows, :], scale_ref[rows, :1], egain_ref[...])
        dpre_ref[rows, :] = (dot_t(dsum.astype(BF), wo_ref[...]) * pre_ref[rows, :]).astype(BF)

    back += start_copies([(dpre_ref, dpre_out)], sems, done + 2)
    dpre = dpre_ref[...]
    hub_sums_ref[...] = times(dot(hot_cols(ids_ref[0:1, :], slots, hub_count), dpre), ws_ref)
    back += start_copies([(hub_sums_ref, hub_sums_out)], sems, done + 3)
    gathered_ref[...] = dot(hot_cols(ids_ref[0:1, :], 0, slots), dpre)
    back += start_copies([(gathered_ref.at[pl.ds(RIM, node_count)], own_out)], sems, done + 4)
    start = pl.multiple_of(core_ref[0] * (RIM + node_count), 16)
    rim_ref[...] = times(gathered_ref[pl.ds(start, RIM), :], ws_ref)
    for copy in back:
        copy.wait()


def late_kernel(
    core_ref, dpre_in, ids_ref, gg_in, ndpre_in, own_in, cot_in, we_in, ws_in, wr_in, win_in,
    egrad_ref, base_ref,
    dpre_ref, gg_ref, ndpre_ref, own_ref, cot_ref, we_ref, ws_ref, wr_ref, win_ref,
    high_ref, low_ref, sems,
):
    node_count, width = cot_in.shape
    slots = 2 * RIM + node_count
    own = slice(RIM, RIM + node_count)
    half = egrad_ref.shape[0]
    copies = start_copies(
        [
            (gg_in, gg_ref),
            (dpre_in, dpre_ref),
            (we_in, we_ref),
            (ndpre_in, ndpre_ref),
            (own_in, own_ref),
            (cot_in, cot_ref),
            (win_in.at[pl.ds(0, width)], win_ref),
            (ws_in, ws_ref),
            (wr_in, wr_ref),
        ],
        sems,
    )
    for copy in copies:
        copy.wait()
    high, low = split2(gg_ref[...])
    for ref, part in ((high_ref, high), (low_ref, low)):
        ref[...] = jnp.zeros_like(ref)
        ref[own] = part
    rows = pl.ds(pl.multiple_of(core_ref[0] * half, half), half)
    hot = hot_rows(ids_ref[1:2, rows], 0, slots)
    upstream = dot(hot, high_ref[...]) + dot(hot, low_ref[...])
    egrad_ref[...] = (upstream + dot_t(dpre_ref[rows, :], we_ref[...])).astype(BF)
    base = cot_ref[...].astype(F32) + dot_t(ndpre_ref[...], win_ref[...])
    recv = dot(hot_cols(ids_ref[1:2, :], RIM, node_count), dpre_ref[...])
    for sums, weight in ((own_ref[...], ws_ref), (recv, wr_ref)):
        high, low = split2(sums)
        base += dot_t(high, weight[...]) + dot_t(low, weight[...])
    base_ref[...] = base


def last_kernel(hub_ref, rims_in, base_in, out_ref, rims_ref, base_ref, sems):
    node_count = base_in.shape[0]
    copies = start_copies([(rims_in, rims_ref), (base_in, base_ref)], sems)
    hub = hub_ref[0]
    for z in range(1, hub_ref.shape[0]):
        hub += hub_ref[z]
    for copy in copies:
        copy.wait()
    base_ref[:RIM] += rims_ref[RIM:].astype(F32)
    base_ref[node_count - RIM :] += rims_ref[:RIM].astype(F32)
    for r in range(HUB_DEV):
        base_ref[r : r + 1] += jnp.concatenate(
            [hub[4 * r + j : 4 * r + j + 1] for j in range(4)], axis=1
        )
    out_ref[...] = base_ref[...].astype(BF)


def both_ways(x, step):
    count = math.prod(lax.axis_size(a) for a in SPACE)
    pairs = [
        (2 * i + c, 2 * (i + d) + c)
        for i in range(count)
        for c, d in ((0, step), (1, -step))
        if 0 <= i + d < count
    ]
    return lax.ppermute(x, ALL, pairs)


def layer(
    nodes,
    edges,
    senders,
    receivers,
    edge_proj,
    send_proj,
    recv_proj,
    edge_bias,
    edge_out,
    edge_gain,
    edge_shift,
    node_in,
    node_bias,
    node_out,
    node_gain,
    node_shift,
    node_cot,
):
    node_count, width = nodes.shape
    half = edges.shape[0]
    edge_count = 2 * half
    steps = edge_count // TILE
    ny, nz, nx = (lax.axis_size(a) for a in SPACE)
    plane = ny * nx
    hub_count = plane * HUB_DEV * nz
    slots = 2 * RIM + node_count
    core = lax.axis_index("c").astype(I32)
    own_block = lax.axis_index(SPACE)
    row = lambda v: (v.reshape(1, width), VM)
    wide = lambda rows, kind=BF: pltpu.VMEM((rows, width), kind)
    square = 2 * width * width

    my_hub, my_rim = call(
        prep_kernel,
        [(core.reshape(1), SM), (nodes, HB)],
        [((nz, 8, LANES), F32, VM), ((RIM, width), BF, VM)],
        [wide(16)],
        copies=2,
    )
    rim = both_ways(my_rim, 1)
    by_z = lax.all_to_all(my_hub, "z", 0, 0)
    (spread,) = call(
        spread_kernel,
        [(by_z.reshape(nz * 8, LANES), VM)],
        [((plane, HUB_DEV * nz, width), BF, VM)],
        room=54000,
    )
    hubs = lax.all_to_all(spread, PLANE, 0, 0).reshape(hub_count, width)

    rims = lax.all_gather(rim, "c", axis=0, tiled=True)
    other = lax.ppermute(edges, "c", [(0, 1), (1, 0)])
    ids = lax.all_gather(jnp.stack([senders, receivers]), "c", axis=1, tiled=True)
    block = ids[0] // node_count
    line = ids[0] - block * node_count
    hub_y, hub_zx = block // (nz * nx), block % (nz * nx)
    hub_z, hub_x = hub_zx // nx, hub_zx % nx
    hub_slot = ((hub_y * nx + hub_x) * HUB_DEV + line) * nz + hub_z
    slot = jnp.where(
        block == own_block,
        RIM + line,
        jnp.where(
            (block == own_block - 1) & (line >= node_count - RIM),
            line - (node_count - RIM),
            jnp.where(
                (block == own_block + 1) & (line < RIM),
                RIM + node_count + line,
                slots + hub_slot,
            ),
        ),
    )
    ids = jnp.stack([slot, ids[1] - own_block * node_count + RIM])

    (near,) = call(
        near_kernel,
        [
            (core.reshape(1), SM), (edges, HB), (other, HB), (ids, VM), (nodes, HB), (rims, HB),
            (edge_proj, HB), (send_proj, HB), (recv_proj, HB), row(edge_bias),
        ],
        [((edge_count, width), F32, HB)],
        [wide(edge_count)] + [wide(slots)] + [wide(width)] * 3 + [wide(slots)] * 2
        + [wide(edge_count, F32)],
        copies=8 + steps,
        flops=square * (edge_count * 2 + 2 * slots),
    )
    new_nodes, dpre, hub_sums, my_rim, own_sums, gathered_grad, node_dpre = call(
        main_kernel,
        [
            (core.reshape(1), SM), (hubs, HB), (near, HB), (edges, HB), (other, HB), (ids, VM),
            (nodes, HB), (node_cot, HB), (send_proj, HB), (edge_out, HB), (node_in, HB), (node_out, HB),
            row(edge_gain), row(edge_shift), row(node_bias), row(node_gain), row(node_shift),
        ],
        [
            ((node_count, width), BF, VM),
            ((edge_count, width), BF, HB),
            ((hub_count, width), BF, HB),
            ((RIM, width), BF, VM),
            ((node_count, width), F32, HB),
            ((node_count, width), F32, HB),
            ((node_count, width), BF, HB),
        ],
        [wide(hub_count), wide(edge_count, F32), wide(edge_count)]
        + [wide(node_count)] * 2 + [wide(width)] * 2 + [wide(2 * width), wide(width)]
        + [wide(edge_count), wide(hub_count), wide(node_count, F32), wide(node_count)]
        + [wide(hub_count), wide(edge_count, F32), pltpu.VMEM((edge_count, LANES), F32)]
        + [wide(slots, F32), wide(slots), wide(slots)],
        copies=14 + steps,
        flops=square * (edge_count * 6 + hub_count),
        room=0,
    )

    hub_back = lax.all_to_all(hub_sums.reshape(plane, HUB_DEV * nz, width), PLANE, 0, 0)
    rim = both_ways(my_rim, -1)
    edge_grad, base = call(
        late_kernel,
        [
            (core.reshape(1), SM), (dpre, HB), (ids, VM), (gathered_grad, HB), (node_dpre, HB),
            (own_sums, HB), (node_cot, HB), (edge_proj, HB), (send_proj, HB), (recv_proj, HB),
            (node_in, HB),
        ],
        [((half, width), BF, VM), ((node_count, width), F32, VM)],
        [wide(edge_count), wide(node_count, F32), wide(node_count), wide(node_count, F32)]
        + [wide(node_count)] + [wide(width)] * 4 + [wide(slots)] * 2,
        copies=9,
        flops=square * edge_count * 2,
    )
    (by_z,) = call(
        gather_kernel,
        [(hub_back, HB)],
        [((nz * 8, LANES), F32, VM)],
        [pltpu.VMEM((plane, HUB_DEV * nz, width), BF)],
        copies=4,
        room=54000,
    )
    hub_back = lax.all_to_all(by_z.reshape(nz, 8, LANES), "z", 0, 0)
    rims = lax.all_gather(rim, "c", axis=0, tiled=True)
    (node_grad,) = call(
        last_kernel,
        [(hub_back, VM), (rims, HB), (base, HB)],
        [((node_count, width), BF, VM)],
        [wide(2 * RIM), wide(node_count, F32)],
        copies=2,
        room=0,
    )
    return new_nodes, node_grad, edge_grad


def solution(mesh):
    fine = Mesh(np.asarray(mesh.devices).reshape(*SHAPE, 2), ALL)
    rows, both = P(SPACE, None), P(ALL, None)
    whole = P()
    in_specs = (rows, both, P(ALL), P(ALL)) + (whole,) * 12 + (rows,)
    return jax.shard_map(
        layer, mesh=fine, in_specs=in_specs, out_specs=(rows, rows, both), check_vma=False
    )
```

```python
import math

import jax
import jax.numpy as jnp
import numpy as np
from jax import lax
from jax.experimental import pallas as pl
from jax.experimental.pallas import tpu as pltpu
from jax.sharding import Mesh, PartitionSpec as P

RIM = 48
HUB_DEV = 2
EPS = 1e-05
BF = jnp.bfloat16
F32 = jnp.float32
I32 = jnp.int32
ALL = ("y", "z", "x", "c")
SPACE = ("y", "z", "x")
PLANE = ("y", "x")
LANES = 128
TILE = 256
SHAPE = (4, 16, 4)
GRANT = 60 * 1024 * 1024


def dot(a, b):
    return jnp.dot(a, b, preferred_element_type=F32)


def dot_t(a, b):
    return lax.dot_general(a, b, (((1,), (1,)), ((), ())), preferred_element_type=F32)


def split2(v):
    high = v.astype(BF)
    return high, (v - high.astype(F32)).astype(BF)


def times(sums, weight_ref):
    high, low = split2(sums)
    return (dot_t(high, weight_ref[...]) + dot_t(low, weight_ref[...])).astype(BF)


def row_mean(v):
    return jnp.mean(v, axis=-1, keepdims=True)


def layer_stats(values):
    centred = values - row_mean(values)
    inv_scale = lax.rsqrt(row_mean(centred * centred) + EPS)
    return centred * inv_scale, inv_scale


def norm_back(upstream, normed, inv_scale, gain_vec):
    scaled = upstream * gain_vec
    return inv_scale * (scaled - row_mean(scaled) - normed * row_mean(scaled * normed))


def hot_rows(ids, first, count):
    edges = ids.shape[1]
    column = jnp.broadcast_to(ids - first, (LANES, edges)).T
    lane = lax.broadcasted_iota(I32, (edges, LANES), 1)
    parts = [
        jnp.where(column == lane + k, 1.0, 0.0).astype(BF) for k in range(0, count, LANES)
    ]
    return jnp.concatenate(parts, axis=1)[:, :count]


def hot_cols(ids, first, count):
    edges = ids.shape[1]
    slot = lax.broadcasted_iota(I32, (count, edges), 0)
    return jnp.where(slot == ids - first, 1.0, 0.0).astype(BF)


VM = pl.BlockSpec(memory_space=pltpu.VMEM)
SM = pl.BlockSpec(memory_space=pltpu.SMEM)
HB = pl.BlockSpec(memory_space=pltpu.HBM)


def call(kernel, ins, outs, scratch=(), copies=0, flops=0, room=0, aliases=None):
    shapes = [jax.ShapeDtypeStruct(s, d) for s, d, _ in outs]
    args = [a for a, _ in ins]
    moved = sum(math.prod(o.shape) * o.dtype.itemsize for o in shapes + args)
    scratch = list(scratch)
    if copies:
        scratch.append(pltpu.SemaphoreType.DMA((copies,)))
    return pl.pallas_call(
        kernel,
        out_shape=shapes,
        in_specs=[spec for _, spec in ins],
        out_specs=[spec for _, _, spec in outs],
        scratch_shapes=scratch,
        input_output_aliases=aliases or {},
        compiler_params=pltpu.CompilerParams(vmem_limit_bytes=GRANT - room * 1024),
        cost_estimate=pl.CostEstimate(flops=flops, bytes_accessed=moved, transcendentals=0),
    )(*args)


def edge_pairs(core_ref, own_in, other_in, edges_ref):
    half = own_in.shape[0]
    return [
        (src, edges_ref.at[pl.ds(pl.multiple_of(at * half, half), half)])
        for src, at in ((own_in, core_ref[0]), (other_in, 1 - core_ref[0]))
    ]


def start_copies(pairs, sems, first=0):
    copies = [
        pltpu.make_async_copy(src, dst, sems.at[first + k]) for k, (src, dst) in enumerate(pairs)
    ]
    for copy in copies:
        copy.start()
    return copies


def prep_kernel(core_ref, nodes_ref, hub_ref, rim_ref, head_ref, sems):
    node_count = nodes_ref.shape[0]
    start = pl.multiple_of((1 - core_ref[0]) * (node_count - RIM), 16)
    head, rim = start_copies(
        [(nodes_ref.at[:16], head_ref), (nodes_ref.at[pl.ds(start, RIM)], rim_ref)], sems
    )
    head.wait()
    rows = head_ref[...].astype(F32)
    tile = jnp.concatenate(
        [rows[r : r + 1, j * LANES : (j + 1) * LANES] for r in range(HUB_DEV) for j in range(4)],
        axis=0,
    )
    for z in range(hub_ref.shape[0]):
        hub_ref[z] = tile
    rim.wait()


def spread_kernel(rows_ref, out_ref):
    nz = rows_ref.shape[0] // 8
    parts = []
    for r in range(HUB_DEV):
        lanes = [rows_ref[pl.ds(4 * r + j, nz, stride=8), :] for j in range(4)]
        parts.append(jnp.concatenate(lanes, axis=1))
    rows = jnp.concatenate(parts, axis=0).astype(BF)
    for p in range(out_ref.shape[0]):
        out_ref[p] = rows


def gather_kernel(sums_ref, out_ref, buf_ref, sems):
    planes = sums_ref.shape[0]
    nz = out_ref.shape[0] // 8
    quarter = planes // 4
    pairs = [
        (sums_ref.at[pl.ds(k * quarter, quarter)], buf_ref.at[pl.ds(k * quarter, quarter)])
        for k in range(4)
    ]
    copies = start_copies(pairs, sems)
    total = jnp.zeros(buf_ref.shape[1:], F32)
    for p in range(planes):
        if p % quarter == 0:
            copies[p // quarter].wait()
        total += buf_ref[p].astype(F32)
    for r in range(HUB_DEV):
        for j in range(4):
            out_ref[pl.ds(4 * r + j, nz, stride=8), :] = total[:, j * LANES : (j + 1) * LANES]


def near_kernel(
    core_ref, own_in, other_in, ids_ref, nodes_in, rims_in, we_in, ws_in, wr_in, bias_ref,
    pre_out,
    edges_ref, frame_ref, we_ref, ws_ref, wr_ref, send_ref, recv_ref, pre_ref, sems,
):
    node_count = nodes_in.shape[0]
    slots = 2 * RIM + node_count
    copies = start_copies(
        [
            (nodes_in, frame_ref.at[pl.ds(RIM, node_count)]),
            (rims_in.at[pl.ds(0, RIM)], frame_ref.at[pl.ds(0, RIM)]),
            (rims_in.at[pl.ds(RIM, RIM)], frame_ref.at[pl.ds(RIM + node_count, RIM)]),
            (ws_in, ws_ref),
            (wr_in, wr_ref),
            (we_in, we_ref),
        ]
        + edge_pairs(core_ref, own_in, other_in, edges_ref),
        sems,
    )
    for copy in copies[:4]:
        copy.wait()
    send_ref[...] = dot(frame_ref[...], ws_ref[...]).astype(BF)
    copies[4].wait()
    recv_ref[...] = dot(frame_ref[...], wr_ref[...]).astype(BF)
    for copy in copies[5:]:
        copy.wait()
    back = []
    for i in range(edges_ref.shape[0] // TILE):
        rows = pl.ds(i * TILE, TILE)
        pre = dot(edges_ref[rows, :], we_ref[...])
        pre += dot(hot_rows(ids_ref[0:1, rows], 0, slots), send_ref[...])
        pre += dot(hot_rows(ids_ref[1:2, rows], 0, slots), recv_ref[...])
        pre_ref[rows, :] = pre + bias_ref[...]
        back += start_copies([(pre_ref.at[rows], pre_out.at[rows])], sems, len(copies) + i)
    for copy in back:
        copy.wait()


def main_kernel(
    core_ref, hubs_in, pre_in, own_in, other_in, ids_ref, nodes_in, cot_in, ws_in, wo_in, win_in, wout_in,
    egain_ref, eshift_ref, nbias_ref, ngain_ref, nshift_ref,
    new_ref, dpre_out, hub_sums_out, rim_ref, own_out, gg_out, ndpre_out,
    hubs_ref, pre_ref, edges_ref, nodes_ref, cot_ref, ws_ref, wo_ref, win_ref, wout_ref,
    dpre_ref, hub_sums_ref, gg_ref, ndpre_ref,
    terms_ref, normed_ref, scale_ref, gathered_ref, high_ref, low_ref, sems,
):
    node_count, width = nodes_in.shape
    hub_count = hubs_in.shape[0]
    edge_count = edges_ref.shape[0]
    steps = edge_count // TILE
    slots = 2 * RIM + node_count
    own = slice(RIM, RIM + node_count)
    tiles = [pl.ds(i * TILE, TILE) for i in range(steps)]
    hubs, ws, wo, *rest = start_copies(
        [(hubs_in, hubs_ref), (ws_in, ws_ref), (wo_in, wo_ref)]
        + [(pre_in.at[rows], pre_ref.at[rows]) for rows in tiles]
        + edge_pairs(core_ref, own_in, other_in, edges_ref)
        + [(nodes_in, nodes_ref), (cot_in, cot_ref), (win_in, win_ref), (wout_in, wout_ref)],
        sems,
    )
    done = 3 + len(rest)
    gathered_ref[...] = jnp.zeros_like(gathered_ref)
    hubs.wait()
    ws.wait()
    terms_ref[...] = dot(hubs_ref[...], ws_ref[...]).astype(BF)
    for i, rows in enumerate(tiles):
        rest[i].wait()
        if i == 0:
            wo.wait()
            rest[steps].wait()
            rest[steps + 1].wait()
        pre = pre_ref[rows, :] + dot(hot_rows(ids_ref[0:1, rows], slots, hub_count), terms_ref[...])
        gate = jax.nn.sigmoid(pre)
        pre_ref[rows, :] = gate * (1.0 + pre * (1.0 - gate))
        edge_sum = dot((pre * gate).astype(BF), wo_ref[...])
        normed, scale = layer_stats(edge_sum)
        normed_ref[rows, :] = normed
        scale_ref[rows, :] = jnp.broadcast_to(scale, (TILE, LANES))
        new_edges = edges_ref[rows, :].astype(F32) + normed * egain_ref[...] + eshift_ref[...]
        gathered_ref[...] += dot(hot_cols(ids_ref[1:2, rows], 0, slots), new_edges.astype(BF))

    for copy in rest[steps + 2 :]:
        copy.wait()
    nodes = nodes_ref[...]
    gathered = gathered_ref[own].astype(BF)
    node_pre = dot(nodes, win_ref[:width]) + dot(gathered, win_ref[width:]) + nbias_ref[...]
    gate = jax.nn.sigmoid(node_pre)
    node_mix = dot((node_pre * gate).astype(BF), wout_ref[...])
    normed, scale = layer_stats(node_mix)
    new_nodes = nodes.astype(F32) + normed * ngain_ref[...] + nshift_ref[...]
    new_ref[...] = new_nodes.astype(BF)
    dmix = norm_back(cot_ref[...].astype(F32), normed, scale, ngain_ref[...]).astype(BF)
    ndpre = dot_t(dmix, wout_ref[...]) * (gate * (1.0 + node_pre * (1.0 - gate)))
    ndpre = ndpre.astype(BF)
    ndpre_ref[...] = ndpre
    gathered_grad = dot_t(ndpre, win_ref[width:])
    gg_ref[...] = gathered_grad
    back = start_copies([(ndpre_ref, ndpre_out), (gg_ref, gg_out)], sems, done)
    high, low = split2(gathered_grad)
    for ref, part in ((high_ref, high), (low_ref, low)):
        ref[...] = jnp.zeros_like(ref)
        ref[own] = part

    for rows in tiles:
        hot = hot_rows(ids_ref[1:2, rows], 0, slots)
        upstream = dot(hot, high_ref[...]) + dot(hot, low_ref[...])
        dsum = norm_back(upstream, normed_ref[rows, :], scale_ref[rows, :1], egain_ref[...])
        dpre_ref[rows, :] = (dot_t(dsum.astype(BF), wo_ref[...]) * pre_ref[rows, :]).astype(BF)

    back += start_copies([(dpre_ref, dpre_out)], sems, done + 2)
    dpre = dpre_ref[...]
    hub_sums_ref[...] = times(dot(hot_cols(ids_ref[2:3, :], 0, hub_count // 2), dpre), ws_ref)
    back += start_copies([(hub_sums_ref, hub_sums_out)], sems, done + 3)
    gathered_ref[...] = dot(hot_cols(ids_ref[0:1, :], 0, slots), dpre)
    back += start_copies([(gathered_ref.at[pl.ds(RIM, node_count)], own_out)], sems, done + 4)
    start = pl.multiple_of(core_ref[0] * (RIM + node_count), 16)
    rim_ref[...] = times(gathered_ref[pl.ds(start, RIM), :], ws_ref)
    for copy in back:
        copy.wait()


def late_kernel(
    core_ref, dpre_in, ids_ref, gg_in, ndpre_in, own_in, cot_in, we_in, ws_in, wr_in, win_in,
    egrad_ref, base_ref,
    dpre_ref, gg_ref, ndpre_ref, own_ref, cot_ref, we_ref, ws_ref, wr_ref, win_ref,
    high_ref, low_ref, sems,
):
    node_count, width = cot_in.shape
    slots = 2 * RIM + node_count
    own = slice(RIM, RIM + node_count)
    half = egrad_ref.shape[0]
    copies = start_copies(
        [
            (gg_in, gg_ref),
            (dpre_in, dpre_ref),
            (we_in, we_ref),
            (ndpre_in, ndpre_ref),
            (own_in, own_ref),
            (cot_in, cot_ref),
            (win_in.at[pl.ds(0, width)], win_ref),
            (ws_in, ws_ref),
            (wr_in, wr_ref),
        ],
        sems,
    )
    for copy in copies:
        copy.wait()
    high, low = split2(gg_ref[...])
    for ref, part in ((high_ref, high), (low_ref, low)):
        ref[...] = jnp.zeros_like(ref)
        ref[own] = part
    rows = pl.ds(pl.multiple_of(core_ref[0] * half, half), half)
    hot = hot_rows(ids_ref[1:2, rows], 0, slots)
    upstream = dot(hot, high_ref[...]) + dot(hot, low_ref[...])
    egrad_ref[...] = (upstream + dot_t(dpre_ref[rows, :], we_ref[...])).astype(BF)
    base = cot_ref[...].astype(F32) + dot_t(ndpre_ref[...], win_ref[...])
    recv = dot(hot_cols(ids_ref[1:2, :], RIM, node_count), dpre_ref[...])
    for sums, weight in ((own_ref[...], ws_ref), (recv, wr_ref)):
        high, low = split2(sums)
        base += dot_t(high, weight[...]) + dot_t(low, weight[...])
    base_ref[...] = base


def sum_kernel(rims_in, base_in, out_ref, head_ref, rims_ref, base_ref, sems):
    node_count = base_in.shape[0]
    for copy in start_copies([(rims_in, rims_ref), (base_in, base_ref)], sems):
        copy.wait()
    base_ref[:RIM] += rims_ref[RIM:].astype(F32)
    base_ref[node_count - RIM :] += rims_ref[:RIM].astype(F32)
    head_ref[...] = base_ref[: head_ref.shape[0]]
    out_ref[...] = base_ref[...].astype(BF)


def last_kernel(hub_ref, head_ref, grad_in, out_ref, rows_ref, sum_ref, sems):
    del grad_in
    hub = hub_ref[0:8]
    for z in range(1, hub_ref.shape[0] // 8):
        hub += hub_ref[8 * z : 8 * z + 8]
    sum_ref[...] = head_ref[...]
    for r in range(HUB_DEV):
        sum_ref[r : r + 1] += jnp.concatenate(
            [hub[4 * r + j : 4 * r + j + 1] for j in range(4)], axis=1
        )
    rows_ref[...] = sum_ref[...].astype(BF)
    (copy,) = start_copies([(rows_ref, out_ref.at[pl.ds(0, rows_ref.shape[0])])], sems)
    copy.wait()


def both_ways(x, step):
    count = math.prod(lax.axis_size(a) for a in SPACE)
    pairs = [
        (2 * i + c, 2 * (i + d) + c)
        for i in range(count)
        for c, d in ((0, step), (1, -step))
        if 0 <= i + d < count
    ]
    return lax.ppermute(x, ALL, pairs)


def layer(
    nodes,
    edges,
    senders,
    receivers,
    edge_proj,
    send_proj,
    recv_proj,
    edge_bias,
    edge_out,
    edge_gain,
    edge_shift,
    node_in,
    node_bias,
    node_out,
    node_gain,
    node_shift,
    node_cot,
):
    node_count, width = nodes.shape
    half = edges.shape[0]
    edge_count = 2 * half
    steps = edge_count // TILE
    ny, nz, nx = (lax.axis_size(a) for a in SPACE)
    plane = ny * nx
    hub_count = plane * HUB_DEV * nz
    slots = 2 * RIM + node_count
    core = lax.axis_index("c").astype(I32)
    own_block = lax.axis_index(SPACE)
    row = lambda v: (v.reshape(1, width), VM)
    wide = lambda rows, kind=BF: pltpu.VMEM((rows, width), kind)
    square = 2 * width * width

    my_hub, my_rim = call(
        prep_kernel,
        [(core.reshape(1), SM), (nodes, HB)],
        [((nz, 8, LANES), F32, VM), ((RIM, width), BF, VM)],
        [wide(16)],
        copies=2,
    )
    rim = both_ways(my_rim, 1)
    by_z = lax.all_to_all(my_hub, "z", 0, 0)
    (spread,) = call(
        spread_kernel,
        [(by_z.reshape(nz * 8, LANES), VM)],
        [((plane, HUB_DEV * nz, width), BF, VM)],
        room=54000,
    )
    hubs = lax.all_to_all(spread, PLANE, 0, 0).reshape(hub_count, width)

    rims = lax.all_gather(rim, "c", axis=0, tiled=True)
    other = lax.ppermute(edges, "c", [(0, 1), (1, 0)])
    ids = lax.all_gather(jnp.stack([senders, receivers]), "c", axis=1, tiled=True)
    block = ids[0] // node_count
    line = ids[0] - block * node_count
    hub_y, hub_zx = block // (nz * nx), block % (nz * nx)
    hub_z, hub_x = hub_zx // nx, hub_zx % nx
    hub_slot = ((hub_y * nx + hub_x) * HUB_DEV + line) * nz + hub_z
    from_own = block == own_block
    from_left = (block == own_block - 1) & (line >= node_count - RIM)
    from_right = (block == own_block + 1) & (line < RIM)
    slot = jnp.where(
        from_own,
        RIM + line,
        jnp.where(
            from_left,
            line - (node_count - RIM),
            jnp.where(from_right, RIM + node_count + line, slots + hub_slot),
        ),
    )
    near_by = from_own | from_left | from_right
    hub_sent = jnp.where(near_by | (line != core), -1, (hub_y * nx + hub_x) * nz + hub_z)
    ids = jnp.stack([slot, ids[1] - own_block * node_count + RIM, hub_sent])

    (near,) = call(
        near_kernel,
        [
            (core.reshape(1), SM), (edges, HB), (other, HB), (ids, VM), (nodes, HB), (rims, HB),
            (edge_proj, HB), (send_proj, HB), (recv_proj, HB), row(edge_bias),
        ],
        [((edge_count, width), F32, HB)],
        [wide(edge_count)] + [wide(slots)] + [wide(width)] * 3 + [wide(slots)] * 2
        + [wide(edge_count, F32)],
        copies=8 + steps,
        flops=square * (edge_count * 2 + 2 * slots),
    )
    new_nodes, dpre, hub_sums, my_rim, own_sums, gathered_grad, node_dpre = call(
        main_kernel,
        [
            (core.reshape(1), SM), (hubs, HB), (near, HB), (edges, HB), (other, HB), (ids, VM),
            (nodes, HB), (node_cot, HB), (send_proj, HB), (edge_out, HB), (node_in, HB), (node_out, HB),
            row(edge_gain), row(edge_shift), row(node_bias), row(node_gain), row(node_shift),
        ],
        [
            ((node_count, width), BF, VM),
            ((edge_count, width), BF, HB),
            ((hub_count // 2, width), BF, HB),
            ((RIM, width), BF, VM),
            ((node_count, width), F32, HB),
            ((node_count, width), F32, HB),
            ((node_count, width), BF, HB),
        ],
        [wide(hub_count), wide(edge_count, F32), wide(edge_count)]
        + [wide(node_count)] * 2 + [wide(width)] * 2 + [wide(2 * width), wide(width)]
        + [wide(edge_count), wide(hub_count // 2), wide(node_count, F32), wide(node_count)]
        + [wide(hub_count), wide(edge_count, F32), pltpu.VMEM((edge_count, LANES), F32)]
        + [wide(slots, F32), wide(slots), wide(slots)],
        copies=14 + steps,
        flops=square * (edge_count * 6 + hub_count),
        room=0,
    )

    hub_back = lax.all_to_all(hub_sums.reshape(plane, nz, width), PLANE, 0, 0)
    rim = both_ways(my_rim, -1)
    edge_grad, base = call(
        late_kernel,
        [
            (core.reshape(1), SM), (dpre, HB), (ids, VM), (gathered_grad, HB), (node_dpre, HB),
            (own_sums, HB), (node_cot, HB), (edge_proj, HB), (send_proj, HB), (recv_proj, HB),
            (node_in, HB),
        ],
        [((half, width), BF, VM), ((node_count, width), F32, VM)],
        [wide(edge_count), wide(node_count, F32), wide(node_count), wide(node_count, F32)]
        + [wide(node_count)] + [wide(width)] * 4 + [wide(slots)] * 2,
        copies=9,
        flops=square * edge_count * 2,
    )
    (by_z,) = call(
        gather_kernel,
        [(hub_back, HB)],
        [((nz * 8, LANES), F32, VM)],
        [pltpu.VMEM((plane, nz, width), BF)],
        copies=4,
        room=54000,
    )
    hub_back = lax.all_to_all(by_z.reshape(2 * nz, 4, LANES), ("z", "c"), 0, 0)
    rims = lax.all_gather(rim, "c", axis=0, tiled=True)
    node_grad, head = call(
        sum_kernel,
        [(rims, HB), (base, HB)],
        [((node_count, width), BF, VM), ((16, width), F32, VM)],
        [wide(2 * RIM), wide(node_count, F32)],
        copies=2,
    )
    (node_grad,) = call(
        last_kernel,
        [(hub_back.reshape(nz * 8, LANES), VM), (head, VM), (node_grad, HB)],
        [((node_count, width), BF, HB)],
        [wide(16), wide(16, F32)],
        copies=1,
        room=54000,
        aliases={2: 0},
    )
    return new_nodes, node_grad, edge_grad


def solution(mesh):
    fine = Mesh(np.asarray(mesh.devices).reshape(*SHAPE, 2), ALL)
    rows, both = P(SPACE, None), P(ALL, None)
    whole = P()
    in_specs = (rows, both, P(ALL), P(ALL)) + (whole,) * 12 + (rows,)
    return jax.shard_map(
        layer, mesh=fine, in_specs=in_specs, out_specs=(rows, rows, both), check_vma=False
    )
```

```python
import math

import jax
import jax.numpy as jnp
import numpy as np
from jax import lax
from jax.experimental import pallas as pl
from jax.experimental.pallas import tpu as pltpu
from jax.sharding import Mesh, PartitionSpec as P

RIM = 48
HUB_DEV = 2
EPS = 1e-05
BF = jnp.bfloat16
F32 = jnp.float32
I32 = jnp.int32
ALL = ("y", "z", "x", "c")
SPACE = ("y", "z", "x")
PLANE = ("y", "x")
LANES = 128
NEAR_TILE = 384
MAIN_TILE = 768
SHAPE = (4, 16, 4)
GRANT = 60 * 1024 * 1024


def dot(a, b):
    return jnp.dot(a, b, preferred_element_type=F32)


def dot_t(a, b):
    return lax.dot_general(a, b, (((1,), (1,)), ((), ())), preferred_element_type=F32)


def split2(v):
    high = v.astype(BF)
    return high, (v - high.astype(F32)).astype(BF)


def times(sums, weight_ref):
    high, low = split2(sums)
    return (dot_t(high, weight_ref[...]) + dot_t(low, weight_ref[...])).astype(BF)


def row_mean(v):
    return jnp.mean(v, axis=-1, keepdims=True)


def layer_stats(values):
    centred = values - row_mean(values)
    inv_scale = lax.rsqrt(row_mean(centred * centred) + EPS)
    return centred * inv_scale, inv_scale


def norm_back(upstream, normed, inv_scale, gain_vec):
    scaled = upstream * gain_vec
    return inv_scale * (scaled - row_mean(scaled) - normed * row_mean(scaled * normed))


def hot_rows(ids, first, count):
    edges = ids.shape[1]
    column = jnp.broadcast_to(ids - first, (LANES, edges)).T
    lane = lax.broadcasted_iota(I32, (edges, LANES), 1)
    parts = [
        jnp.where(column == lane + k, 1.0, 0.0).astype(BF) for k in range(0, count, LANES)
    ]
    return jnp.concatenate(parts, axis=1)[:, :count]


def hot_cols(ids, first, count):
    edges = ids.shape[1]
    slot = lax.broadcasted_iota(I32, (count, edges), 0)
    return jnp.where(slot == ids - first, 1.0, 0.0).astype(BF)


VM = pl.BlockSpec(memory_space=pltpu.VMEM)
SM = pl.BlockSpec(memory_space=pltpu.SMEM)
HB = pl.BlockSpec(memory_space=pltpu.HBM)


def call(kernel, ins, outs, scratch=(), copies=0, flops=0, room=0, aliases=None):
    shapes = [jax.ShapeDtypeStruct(s, d) for s, d, _ in outs]
    args = [a for a, _ in ins]
    moved = sum(math.prod(o.shape) * o.dtype.itemsize for o in shapes + args)
    scratch = list(scratch)
    if copies:
        scratch.append(pltpu.SemaphoreType.DMA((copies,)))
    return pl.pallas_call(
        kernel,
        out_shape=shapes,
        in_specs=[spec for _, spec in ins],
        out_specs=[spec for _, _, spec in outs],
        scratch_shapes=scratch,
        input_output_aliases=aliases or {},
        compiler_params=pltpu.CompilerParams(vmem_limit_bytes=GRANT - room * 1024),
        cost_estimate=pl.CostEstimate(flops=flops, bytes_accessed=moved, transcendentals=0),
    )(*args)


def edge_pairs(core_ref, own_in, other_in, edges_ref):
    half = own_in.shape[0]
    return [
        (src, edges_ref.at[pl.ds(pl.multiple_of(at * half, half), half)])
        for src, at in ((own_in, core_ref[0]), (other_in, 1 - core_ref[0]))
    ]


def start_copies(pairs, sems, first=0):
    copies = [
        pltpu.make_async_copy(src, dst, sems.at[first + k]) for k, (src, dst) in enumerate(pairs)
    ]
    for copy in copies:
        copy.start()
    return copies


def prep_kernel(core_ref, nodes_ref, hub_ref, rim_ref, head_ref, sems):
    node_count = nodes_ref.shape[0]
    start = pl.multiple_of((1 - core_ref[0]) * (node_count - RIM), 16)
    head, rim = start_copies(
        [(nodes_ref.at[:16], head_ref), (nodes_ref.at[pl.ds(start, RIM)], rim_ref)], sems
    )
    head.wait()
    rows = head_ref[...].astype(F32)
    tile = jnp.concatenate(
        [rows[r : r + 1, j * LANES : (j + 1) * LANES] for r in range(HUB_DEV) for j in range(4)],
        axis=0,
    )
    for z in range(hub_ref.shape[0]):
        hub_ref[z] = tile
    rim.wait()


def spread_kernel(rows_ref, out_ref):
    nz = rows_ref.shape[0] // 8
    parts = []
    for r in range(HUB_DEV):
        lanes = [rows_ref[pl.ds(4 * r + j, nz, stride=8), :] for j in range(4)]
        parts.append(jnp.concatenate(lanes, axis=1))
    rows = jnp.concatenate(parts, axis=0).astype(BF)
    for p in range(out_ref.shape[0]):
        out_ref[p] = rows


def gather_kernel(sums_ref, out_ref, buf_ref, sems):
    planes = sums_ref.shape[0]
    nz = out_ref.shape[0] // 4
    quarter = planes // 4
    pairs = [
        (sums_ref.at[pl.ds(k * quarter, quarter)], buf_ref.at[pl.ds(k * quarter, quarter)])
        for k in range(4)
    ]
    copies = start_copies(pairs, sems)
    total = jnp.zeros(buf_ref.shape[1:], F32)
    for p in range(planes):
        if p % quarter == 0:
            copies[p // quarter].wait()
        total += buf_ref[p].astype(F32)
    for j in range(4):
        out_ref[pl.ds(j, nz, stride=4), :] = total[:, j * LANES : (j + 1) * LANES]


def near_kernel(
    core_ref, own_in, other_in, ids_ref, nodes_in, rims_in, we_in, ws_in, wr_in, bias_ref,
    pre_out,
    edges_ref, frame_ref, we_ref, ws_ref, wr_ref, send_ref, recv_ref, pre_ref, sems,
):
    node_count = nodes_in.shape[0]
    slots = 2 * RIM + node_count
    copies = start_copies(
        [
            (nodes_in, frame_ref.at[pl.ds(RIM, node_count)]),
            (rims_in.at[pl.ds(0, RIM)], frame_ref.at[pl.ds(0, RIM)]),
            (rims_in.at[pl.ds(RIM, RIM)], frame_ref.at[pl.ds(RIM + node_count, RIM)]),
            (ws_in, ws_ref),
            (wr_in, wr_ref),
            (we_in, we_ref),
        ]
        + edge_pairs(core_ref, own_in, other_in, edges_ref),
        sems,
    )
    for copy in copies[:4]:
        copy.wait()
    send_ref[...] = dot(frame_ref[...], ws_ref[...]).astype(BF)
    copies[4].wait()
    recv_ref[...] = dot(frame_ref[...], wr_ref[...]).astype(BF)
    for copy in copies[5:]:
        copy.wait()
    back = []
    for i in range(edges_ref.shape[0] // NEAR_TILE):
        rows = pl.ds(i * NEAR_TILE, NEAR_TILE)
        pre = dot(edges_ref[rows, :], we_ref[...])
        pre += dot(hot_rows(ids_ref[0:1, rows], 0, slots), send_ref[...])
        pre += dot(hot_rows(ids_ref[1:2, rows], 0, slots), recv_ref[...])
        pre_ref[rows, :] = pre + bias_ref[...]
        back += start_copies([(pre_ref.at[rows], pre_out.at[rows])], sems, len(copies) + i)
    for copy in back:
        copy.wait()


def main_kernel(
    core_ref, hubs_in, pre_in, own_in, other_in, ids_ref, nodes_in, cot_in, ws_in, wo_in, win_in, wout_in,
    egain_ref, eshift_ref, nbias_ref, ngain_ref, nshift_ref,
    new_ref, dpre_out, hub_sums_out, rim_ref, own_out, gg_out, ndpre_out,
    hubs_ref, pre_ref, edges_ref, nodes_ref, cot_ref, ws_ref, wo_ref, win_ref, wout_ref,
    dpre_ref, hub_sums_ref, gg_ref, ndpre_ref,
    terms_ref, normed_ref, scale_ref, gathered_ref, high_ref, low_ref, sems,
):
    node_count, width = nodes_in.shape
    hub_count = hubs_in.shape[0]
    edge_count = edges_ref.shape[0]
    steps = edge_count // MAIN_TILE
    slots = 2 * RIM + node_count
    own = slice(RIM, RIM + node_count)
    tiles = [pl.ds(i * MAIN_TILE, MAIN_TILE) for i in range(steps)]
    hubs, ws, wo, *rest = start_copies(
        [(hubs_in, hubs_ref), (ws_in, ws_ref), (wo_in, wo_ref)]
        + [(pre_in.at[rows], pre_ref.at[rows]) for rows in tiles]
        + edge_pairs(core_ref, own_in, other_in, edges_ref)
        + [(nodes_in, nodes_ref), (cot_in, cot_ref), (win_in, win_ref), (wout_in, wout_ref)],
        sems,
    )
    done = 3 + len(rest)
    gathered_ref[...] = jnp.zeros_like(gathered_ref)
    hubs.wait()
    ws.wait()
    terms_ref[...] = dot(hubs_ref[...], ws_ref[...]).astype(BF)
    for i, rows in enumerate(tiles):
        rest[i].wait()
        if i == 0:
            wo.wait()
            rest[steps].wait()
            rest[steps + 1].wait()
        pre = pre_ref[rows, :] + dot(hot_rows(ids_ref[0:1, rows], slots, hub_count), terms_ref[...])
        gate = jax.nn.sigmoid(pre)
        act = pre * gate
        pre_ref[rows, :] = gate + act * (1.0 - gate)
        edge_sum = dot(act.astype(BF), wo_ref[...])
        normed, scale = layer_stats(edge_sum)
        normed_ref[rows, :] = normed
        scale_ref[rows, :] = jnp.broadcast_to(scale, (MAIN_TILE, LANES))
        new_edges = edges_ref[rows, :].astype(F32) + normed * egain_ref[...] + eshift_ref[...]
        gathered_ref[...] += dot(hot_cols(ids_ref[1:2, rows], 0, slots), new_edges.astype(BF))

    for copy in rest[steps + 2 :]:
        copy.wait()
    nodes = nodes_ref[...]
    gathered = gathered_ref[own].astype(BF)
    node_pre = dot(nodes, win_ref[:width]) + dot(gathered, win_ref[width:]) + nbias_ref[...]
    gate = jax.nn.sigmoid(node_pre)
    act = node_pre * gate
    node_mix = dot(act.astype(BF), wout_ref[...])
    normed, scale = layer_stats(node_mix)
    new_nodes = nodes.astype(F32) + normed * ngain_ref[...] + nshift_ref[...]
    new_ref[...] = new_nodes.astype(BF)
    dmix = norm_back(cot_ref[...].astype(F32), normed, scale, ngain_ref[...]).astype(BF)
    ndpre = dot_t(dmix, wout_ref[...]) * (gate + act * (1.0 - gate))
    ndpre = ndpre.astype(BF)
    ndpre_ref[...] = ndpre
    gathered_grad = dot_t(ndpre, win_ref[width:])
    gg_ref[...] = gathered_grad
    back = start_copies([(ndpre_ref, ndpre_out), (gg_ref, gg_out)], sems, done)
    scaled = gathered_grad * egain_ref[...]
    high, low = split2(scaled - row_mean(scaled))
    for ref, part in ((high_ref, high), (low_ref, low)):
        ref[...] = jnp.zeros_like(ref)
        ref[own] = part

    for rows in tiles:
        hot = hot_rows(ids_ref[1:2, rows], 0, slots)
        scaled = dot(hot, high_ref[...]) + dot(hot, low_ref[...])
        normed = normed_ref[rows, :]
        dsum = scale_ref[rows, :1] * (scaled - normed * row_mean(scaled * normed))
        dpre_ref[rows, :] = (dot_t(dsum.astype(BF), wo_ref[...]) * pre_ref[rows, :]).astype(BF)

    back += start_copies([(dpre_ref, dpre_out)], sems, done + 2)
    dpre = dpre_ref[...]
    hub_sums_ref[...] = times(dot(hot_cols(ids_ref[2:3, :], 0, hub_count // 2), dpre), ws_ref)
    back += start_copies([(hub_sums_ref, hub_sums_out)], sems, done + 3)
    gathered_ref[...] = dot(hot_cols(ids_ref[0:1, :], 0, slots), dpre)
    back += start_copies([(gathered_ref.at[pl.ds(RIM, node_count)], own_out)], sems, done + 4)
    start = pl.multiple_of(core_ref[0] * (RIM + node_count), 16)
    rim_ref[...] = times(gathered_ref[pl.ds(start, RIM), :], ws_ref)
    for copy in back:
        copy.wait()


def late_kernel(
    core_ref, dpre_in, ids_ref, gg_in, ndpre_in, own_in, cot_in, we_in, ws_in, wr_in, win_in, rims_in,
    egrad_ref, grad_ref, head_ref,
    dpre_ref, gg_ref, ndpre_ref, own_ref, cot_ref, we_ref, ws_ref, wr_ref, win_ref, rims_ref,
    high_ref, low_ref, base_ref, sems,
):
    node_count, width = cot_in.shape
    slots = 2 * RIM + node_count
    own = slice(RIM, RIM + node_count)
    half = egrad_ref.shape[0]
    gg, dpre, we, wr, win, ndpre, ws, sums, cot, rims = start_copies(
        [
            (gg_in, gg_ref),
            (dpre_in, dpre_ref),
            (we_in, we_ref),
            (wr_in, wr_ref),
            (win_in.at[pl.ds(0, width)], win_ref),
            (ndpre_in, ndpre_ref),
            (ws_in, ws_ref),
            (own_in, own_ref),
            (cot_in, cot_ref),
            (rims_in, rims_ref),
        ],
        sems,
    )
    gg.wait()
    high, low = split2(gg_ref[...])
    for ref, part in ((high_ref, high), (low_ref, low)):
        ref[...] = jnp.zeros_like(ref)
        ref[own] = part
    rows = pl.ds(pl.multiple_of(core_ref[0] * half, half), half)
    hot = hot_rows(ids_ref[1:2, rows], 0, slots)
    upstream = dot(hot, high_ref[...]) + dot(hot, low_ref[...])
    dpre.wait()
    we.wait()
    egrad_ref[...] = (upstream + dot_t(dpre_ref[rows, :], we_ref[...])).astype(BF)
    recv = dot(hot_cols(ids_ref[1:2, :], RIM, node_count), dpre_ref[...])
    high, low = split2(recv)
    wr.wait()
    base = dot_t(high, wr_ref[...]) + dot_t(low, wr_ref[...])
    for copy in (win, ndpre, ws, sums, cot, rims):
        copy.wait()
    base += dot_t(ndpre_ref[...], win_ref[...])
    high, low = split2(own_ref[...])
    base += dot_t(high, ws_ref[...]) + dot_t(low, ws_ref[...])
    base_ref[...] = base + cot_ref[...].astype(F32)
    base_ref[:RIM] += rims_ref[RIM:].astype(F32)
    base_ref[node_count - RIM :] += rims_ref[:RIM].astype(F32)
    head_ref[...] = base_ref[: head_ref.shape[0]]
    grad_ref[...] = base_ref[...].astype(BF)


def last_kernel(hub_ref, head_ref, grad_in, out_ref, rows_ref, sum_ref, sems):
    del grad_in
    count = hub_ref.shape[0] // HUB_DEV
    sum_ref[...] = head_ref[...]
    for r in range(HUB_DEV):
        pair = hub_ref[r * count : r * count + 8]
        for k in range(8, count, 8):
            pair += hub_ref[r * count + k : r * count + k + 8]
        hub = pair[:4] + pair[4:]
        sum_ref[r : r + 1] += jnp.concatenate([hub[j : j + 1] for j in range(4)], axis=1)
    rows_ref[...] = sum_ref[...].astype(BF)
    (copy,) = start_copies([(rows_ref, out_ref.at[pl.ds(0, rows_ref.shape[0])])], sems)
    copy.wait()


def both_ways(x, step):
    count = math.prod(lax.axis_size(a) for a in SPACE)
    pairs = [
        (2 * i + c, 2 * (i + d) + c)
        for i in range(count)
        for c, d in ((0, step), (1, -step))
        if 0 <= i + d < count
    ]
    return lax.ppermute(x, ALL, pairs)


def layer(
    nodes,
    edges,
    senders,
    receivers,
    edge_proj,
    send_proj,
    recv_proj,
    edge_bias,
    edge_out,
    edge_gain,
    edge_shift,
    node_in,
    node_bias,
    node_out,
    node_gain,
    node_shift,
    node_cot,
):
    node_count, width = nodes.shape
    half = edges.shape[0]
    edge_count = 2 * half
    ny, nz, nx = (lax.axis_size(a) for a in SPACE)
    plane = ny * nx
    hub_count = plane * HUB_DEV * nz
    slots = 2 * RIM + node_count
    core = lax.axis_index("c").astype(I32)
    own_block = lax.axis_index(SPACE)
    row = lambda v: (v.reshape(1, width), VM)
    wide = lambda rows, kind=BF: pltpu.VMEM((rows, width), kind)
    square = 2 * width * width

    my_hub, my_rim = call(
        prep_kernel,
        [(core.reshape(1), SM), (nodes, HB)],
        [((nz, 8, LANES), F32, VM), ((RIM, width), BF, VM)],
        [wide(16)],
        copies=2,
    )
    rim = both_ways(my_rim, 1)
    by_z = lax.all_to_all(my_hub, "z", 0, 0)
    (spread,) = call(
        spread_kernel,
        [(by_z.reshape(nz * 8, LANES), VM)],
        [((plane, HUB_DEV * nz, width), BF, VM)],
        room=54000,
    )
    hubs = lax.all_to_all(spread, PLANE, 0, 0).reshape(hub_count, width)

    rims = lax.all_gather(rim, "c", axis=0, tiled=True)
    other = lax.ppermute(edges, "c", [(0, 1), (1, 0)])
    ids = lax.all_gather(jnp.stack([senders, receivers]), "c", axis=1, tiled=True)
    block = ids[0] // node_count
    line = ids[0] - block * node_count
    hub_y, hub_zx = block // (nz * nx), block % (nz * nx)
    hub_z, hub_x = hub_zx // nx, hub_zx % nx
    hub_slot = ((hub_y * nx + hub_x) * HUB_DEV + line) * nz + hub_z
    from_own = block == own_block
    from_left = (block == own_block - 1) & (line >= node_count - RIM)
    from_right = (block == own_block + 1) & (line < RIM)
    slot = jnp.where(
        from_own,
        RIM + line,
        jnp.where(
            from_left,
            line - (node_count - RIM),
            jnp.where(from_right, RIM + node_count + line, slots + hub_slot),
        ),
    )
    near_by = from_own | from_left | from_right
    hub_sent = jnp.where(near_by | (line != core), -1, (hub_y * nx + hub_x) * nz + hub_z)
    ids = jnp.stack([slot, ids[1] - own_block * node_count + RIM, hub_sent])

    (near,) = call(
        near_kernel,
        [
            (core.reshape(1), SM), (edges, HB), (other, HB), (ids, VM), (nodes, HB), (rims, HB),
            (edge_proj, HB), (send_proj, HB), (recv_proj, HB), row(edge_bias),
        ],
        [((edge_count, width), F32, HB)],
        [wide(edge_count)] + [wide(slots)] + [wide(width)] * 3 + [wide(slots)] * 2
        + [wide(edge_count, F32)],
        copies=8 + edge_count // NEAR_TILE,
        flops=square * (edge_count * 2 + 2 * slots),
    )
    new_nodes, dpre, hub_sums, my_rim, own_sums, gathered_grad, node_dpre = call(
        main_kernel,
        [
            (core.reshape(1), SM), (hubs, HB), (near, HB), (edges, HB), (other, HB), (ids, VM),
            (nodes, HB), (node_cot, HB), (send_proj, HB), (edge_out, HB), (node_in, HB), (node_out, HB),
            row(edge_gain), row(edge_shift), row(node_bias), row(node_gain), row(node_shift),
        ],
        [
            ((node_count, width), BF, VM),
            ((edge_count, width), BF, HB),
            ((hub_count // 2, width), BF, HB),
            ((RIM, width), BF, VM),
            ((node_count, width), F32, HB),
            ((node_count, width), F32, HB),
            ((node_count, width), BF, HB),
        ],
        [wide(hub_count), wide(edge_count, F32), wide(edge_count)]
        + [wide(node_count)] * 2 + [wide(width)] * 2 + [wide(2 * width), wide(width)]
        + [wide(edge_count), wide(hub_count // 2), wide(node_count, F32), wide(node_count)]
        + [wide(hub_count), wide(edge_count, F32), pltpu.VMEM((edge_count, LANES), F32)]
        + [wide(slots, F32), wide(slots), wide(slots)],
        copies=14 + edge_count // MAIN_TILE,
        flops=square * (edge_count * 6 + hub_count),
        room=0,
    )

    hub_back = lax.all_to_all(hub_sums.reshape(plane, nz, width), PLANE, 0, 0)
    rim = both_ways(my_rim, -1)
    (by_z,) = call(
        gather_kernel,
        [(hub_back, HB)],
        [((nz * 4, LANES), F32, VM)],
        [pltpu.VMEM((plane, nz, width), BF)],
        copies=4,
        room=54000,
    )
    hub_back = lax.all_to_all(by_z.reshape(nz, 4, LANES), "z", 0, 0)
    hub_back = lax.all_gather(hub_back.reshape(nz * 4, LANES), "c", axis=0, tiled=True)
    rims = lax.all_gather(rim, "c", axis=0, tiled=True)
    edge_grad, node_grad, head = call(
        late_kernel,
        [
            (core.reshape(1), SM), (dpre, HB), (ids, VM), (gathered_grad, HB), (node_dpre, HB),
            (own_sums, HB), (node_cot, HB), (edge_proj, HB), (send_proj, HB), (recv_proj, HB),
            (node_in, HB), (rims, HB),
        ],
        [((half, width), BF, VM), ((node_count, width), BF, VM), ((16, width), F32, VM)],
        [wide(edge_count), wide(node_count, F32), wide(node_count), wide(node_count, F32)]
        + [wide(node_count)] + [wide(width)] * 4 + [wide(2 * RIM)] + [wide(slots)] * 2
        + [wide(node_count, F32)],
        copies=10,
        flops=square * edge_count * 2,
    )
    (node_grad,) = call(
        last_kernel,
        [(hub_back, VM), (head, VM), (node_grad, HB)],
        [((node_count, width), BF, HB)],
        [wide(16), wide(16, F32)],
        copies=1,
        room=54000,
        aliases={2: 0},
    )
    return new_nodes, node_grad, edge_grad


def solution(mesh):
    fine = Mesh(np.asarray(mesh.devices).reshape(*SHAPE, 2), ALL)
    rows, both = P(SPACE, None), P(ALL, None)
    whole = P()
    in_specs = (rows, both, P(ALL), P(ALL)) + (whole,) * 12 + (rows,)
    return jax.shard_map(
        layer, mesh=fine, in_specs=in_specs, out_specs=(rows, rows, both), check_vma=False
    )
```

```python
import math

import jax
import jax.numpy as jnp
import numpy as np
from jax import lax
from jax.experimental import pallas as pl
from jax.experimental.pallas import tpu as pltpu
from jax.sharding import Mesh, PartitionSpec as P

RIM = 48
HUB_DEV = 2
EPS = 1e-05
BF = jnp.bfloat16
F32 = jnp.float32
I32 = jnp.int32
ALL = ("y", "z", "x", "c")
SPACE = ("y", "z", "x")
PLANE = ("y", "x")
LANES = 128
MAIN_TILE = 768
SHAPE = (4, 16, 4)
GRANT = 60 * 1024 * 1024


def dot(a, b):
    return jnp.dot(a, b, preferred_element_type=F32)


def dot_t(a, b):
    return lax.dot_general(a, b, (((1,), (1,)), ((), ())), preferred_element_type=F32)


def split2(v):
    high = v.astype(BF)
    return high, (v - high.astype(F32)).astype(BF)


def times(sums, weight_ref):
    high, low = split2(sums)
    return (dot_t(high, weight_ref[...]) + dot_t(low, weight_ref[...])).astype(BF)


def row_mean(v):
    return jnp.mean(v, axis=-1, keepdims=True)


def layer_stats(values):
    centred = values - row_mean(values)
    inv_scale = lax.rsqrt(row_mean(centred * centred) + EPS)
    return centred * inv_scale, inv_scale


def norm_back(upstream, normed, inv_scale, gain_vec):
    scaled = upstream * gain_vec
    return inv_scale * (scaled - row_mean(scaled) - normed * row_mean(scaled * normed))


def hot_rows(ids, first, count):
    edges = ids.shape[1]
    column = jnp.broadcast_to(ids - first, (LANES, edges)).T
    lane = lax.broadcasted_iota(I32, (edges, LANES), 1)
    parts = [
        jnp.where(column == lane + k, 1.0, 0.0).astype(BF) for k in range(0, count, LANES)
    ]
    return jnp.concatenate(parts, axis=1)[:, :count]


def hot_cols(ids, first, count):
    edges = ids.shape[1]
    slot = lax.broadcasted_iota(I32, (count, edges), 0)
    return jnp.where(slot == ids - first, 1.0, 0.0).astype(BF)


VM = pl.BlockSpec(memory_space=pltpu.VMEM)
SM = pl.BlockSpec(memory_space=pltpu.SMEM)
HB = pl.BlockSpec(memory_space=pltpu.HBM)


def call(kernel, ins, outs, scratch=(), copies=0, flops=0, room=0, aliases=None):
    shapes = [jax.ShapeDtypeStruct(s, d) for s, d, _ in outs]
    args = [a for a, _ in ins]
    moved = sum(math.prod(o.shape) * o.dtype.itemsize for o in shapes + args)
    scratch = list(scratch)
    if copies:
        scratch.append(pltpu.SemaphoreType.DMA((copies,)))
    return pl.pallas_call(
        kernel,
        out_shape=shapes,
        in_specs=[spec for _, spec in ins],
        out_specs=[spec for _, _, spec in outs],
        scratch_shapes=scratch,
        input_output_aliases=aliases or {},
        compiler_params=pltpu.CompilerParams(vmem_limit_bytes=GRANT - room * 1024),
        cost_estimate=pl.CostEstimate(flops=flops, bytes_accessed=moved, transcendentals=0),
    )(*args)


def edge_pairs(core_ref, own_in, other_in, edges_ref):
    half = own_in.shape[0]
    return [
        (src, edges_ref.at[pl.ds(pl.multiple_of(at * half, half), half)])
        for src, at in ((own_in, core_ref[0]), (other_in, 1 - core_ref[0]))
    ]


def start_copies(pairs, sems, first=0):
    copies = [
        pltpu.make_async_copy(src, dst, sems.at[first + k]) for k, (src, dst) in enumerate(pairs)
    ]
    for copy in copies:
        copy.start()
    return copies


def prep_kernel(core_ref, nodes_ref, hub_ref, rim_ref, head_ref, sems):
    node_count = nodes_ref.shape[0]
    start = pl.multiple_of((1 - core_ref[0]) * (node_count - RIM), 16)
    head, rim = start_copies(
        [(nodes_ref.at[:16], head_ref), (nodes_ref.at[pl.ds(start, RIM)], rim_ref)], sems
    )
    head.wait()
    rows = head_ref[...].astype(F32)
    tile = jnp.concatenate(
        [rows[r : r + 1, j * LANES : (j + 1) * LANES] for r in range(HUB_DEV) for j in range(4)],
        axis=0,
    )
    for z in range(hub_ref.shape[0]):
        hub_ref[z] = tile
    rim.wait()


def spread_kernel(rows_ref, out_ref):
    nz = rows_ref.shape[0] // 8
    parts = []
    for r in range(HUB_DEV):
        lanes = [rows_ref[pl.ds(4 * r + j, nz, stride=8), :] for j in range(4)]
        parts.append(jnp.concatenate(lanes, axis=1))
    rows = jnp.concatenate(parts, axis=0).astype(BF)
    for p in range(out_ref.shape[0]):
        out_ref[p] = rows


def gather_kernel(sums_ref, out_ref, buf_ref, sems):
    planes = sums_ref.shape[0]
    nz = out_ref.shape[0] // 4
    quarter = planes // 4
    pairs = [
        (sums_ref.at[pl.ds(k * quarter, quarter)], buf_ref.at[pl.ds(k * quarter, quarter)])
        for k in range(4)
    ]
    copies = start_copies(pairs, sems)
    total = jnp.zeros(buf_ref.shape[1:], F32)
    for p in range(planes):
        if p % quarter == 0:
            copies[p // quarter].wait()
        total += buf_ref[p].astype(F32)
    for j in range(4):
        out_ref[pl.ds(j, nz, stride=4), :] = total[:, j * LANES : (j + 1) * LANES]


def near_kernel(
    core_ref, own_ref, other_ref, ids_ref, nodes_ref, rims_ref, we_ref, ws_ref, wr_ref, bias_ref,
    pre_ref,
    frame_ref, send_ref, recv_ref,
):
    node_count = nodes_ref.shape[0]
    half = own_ref.shape[0]
    slots = 2 * RIM + node_count
    frame_ref[:RIM] = rims_ref[:RIM]
    frame_ref[RIM : RIM + node_count] = nodes_ref[...]
    frame_ref[RIM + node_count :] = rims_ref[RIM:]
    send_ref[...] = dot(frame_ref[...], ws_ref[...]).astype(BF)
    recv_ref[...] = dot(frame_ref[...], wr_ref[...]).astype(BF)
    for edges_ref, at in ((own_ref, core_ref[0]), (other_ref, 1 - core_ref[0])):
        rows = pl.ds(pl.multiple_of(at * half, half), half)
        pre = dot(edges_ref[...], we_ref[...])
        pre += dot(hot_rows(ids_ref[0:1, rows], 0, slots), send_ref[...])
        pre += dot(hot_rows(ids_ref[1:2, rows], 0, slots), recv_ref[...])
        pre_ref[rows, :] = pre + bias_ref[...]


def main_kernel(
    core_ref, hubs_in, pre_in, own_in, other_in, ids_ref, nodes_in, cot_in, ws_in, wo_in, win_in, wout_in,
    egain_ref, eshift_ref, nbias_ref, ngain_ref, nshift_ref,
    new_ref, dpre_out, hub_sums_out, rim_ref, own_out, gg_out, ndpre_out,
    hubs_ref, pre_ref, edges_ref, nodes_ref, cot_ref, ws_ref, wo_ref, win_ref, wout_ref,
    dpre_ref, hub_sums_ref, gg_ref, ndpre_ref,
    terms_ref, normed_ref, scale_ref, gathered_ref, high_ref, low_ref, sems,
):
    node_count, width = nodes_in.shape
    hub_count = hubs_in.shape[0]
    edge_count = edges_ref.shape[0]
    steps = edge_count // MAIN_TILE
    slots = 2 * RIM + node_count
    own = slice(RIM, RIM + node_count)
    tiles = [pl.ds(i * MAIN_TILE, MAIN_TILE) for i in range(steps)]
    hubs, ws, *rest = start_copies(
        [(hubs_in, hubs_ref), (ws_in, ws_ref)]
        + [(pre_in.at[rows], pre_ref.at[rows]) for rows in tiles]
        + [(wo_in, wo_ref)]
        + edge_pairs(core_ref, own_in, other_in, edges_ref)
        + [(nodes_in, nodes_ref), (cot_in, cot_ref), (win_in, win_ref), (wout_in, wout_ref)],
        sems,
    )
    done = 2 + len(rest)
    gathered_ref[...] = jnp.zeros_like(gathered_ref)
    hubs.wait()
    ws.wait()
    terms_ref[...] = dot(hubs_ref[...], ws_ref[...]).astype(BF)
    for i, rows in enumerate(tiles):
        rest[i].wait()
        if i == 0:
            for copy in rest[steps : steps + 3]:
                copy.wait()
        pre = pre_ref[rows, :] + dot(hot_rows(ids_ref[0:1, rows], slots, hub_count), terms_ref[...])
        gate = jax.nn.sigmoid(pre)
        act = pre * gate
        pre_ref[rows, :] = gate + act * (1.0 - gate)
        edge_sum = dot(act.astype(BF), wo_ref[...])
        normed, scale = layer_stats(edge_sum)
        normed_ref[rows, :] = normed
        scale_ref[rows, :] = jnp.broadcast_to(scale, (MAIN_TILE, LANES))
        new_edges = edges_ref[rows, :].astype(F32) + normed * egain_ref[...] + eshift_ref[...]
        gathered_ref[...] += dot(hot_cols(ids_ref[1:2, rows], 0, slots), new_edges.astype(BF))

    for copy in rest[steps + 3 :]:
        copy.wait()
    nodes = nodes_ref[...]
    gathered = gathered_ref[own].astype(BF)
    node_pre = dot(nodes, win_ref[:width]) + dot(gathered, win_ref[width:]) + nbias_ref[...]
    gate = jax.nn.sigmoid(node_pre)
    act = node_pre * gate
    node_mix = dot(act.astype(BF), wout_ref[...])
    normed, scale = layer_stats(node_mix)
    new_nodes = nodes.astype(F32) + normed * ngain_ref[...] + nshift_ref[...]
    new_ref[...] = new_nodes.astype(BF)
    dmix = norm_back(cot_ref[...].astype(F32), normed, scale, ngain_ref[...]).astype(BF)
    ndpre = dot_t(dmix, wout_ref[...]) * (gate + act * (1.0 - gate))
    ndpre = ndpre.astype(BF)
    ndpre_ref[...] = ndpre
    gathered_grad = dot_t(ndpre, win_ref[width:])
    gg_ref[...] = gathered_grad
    back = start_copies([(ndpre_ref, ndpre_out), (gg_ref, gg_out)], sems, done)
    scaled = gathered_grad * egain_ref[...]
    high, low = split2(scaled - row_mean(scaled))
    for ref, part in ((high_ref, high), (low_ref, low)):
        ref[...] = jnp.zeros_like(ref)
        ref[own] = part

    for rows in tiles:
        hot = hot_rows(ids_ref[1:2, rows], 0, slots)
        scaled = dot(hot, high_ref[...]) + dot(hot, low_ref[...])
        normed = normed_ref[rows, :]
        dsum = scale_ref[rows, :1] * (scaled - normed * row_mean(scaled * normed))
        dpre_ref[rows, :] = (dot_t(dsum.astype(BF), wo_ref[...]) * pre_ref[rows, :]).astype(BF)

    back += start_copies([(dpre_ref, dpre_out)], sems, done + 2)
    dpre = dpre_ref[...]
    hub_sums_ref[...] = times(dot(hot_cols(ids_ref[2:3, :], 0, hub_count // 2), dpre), ws_ref)
    back += start_copies([(hub_sums_ref, hub_sums_out)], sems, done + 3)
    gathered_ref[...] = dot(hot_cols(ids_ref[0:1, :], 0, slots), dpre)
    back += start_copies([(gathered_ref.at[pl.ds(RIM, node_count)], own_out)], sems, done + 4)
    start = pl.multiple_of(core_ref[0] * (RIM + node_count), 16)
    rim_ref[...] = times(gathered_ref[pl.ds(start, RIM), :], ws_ref)
    for copy in back:
        copy.wait()


def late_kernel(
    core_ref, dpre_in, ids_ref, gg_in, ndpre_in, own_in, cot_in, we_in, ws_in, wr_in, win_in, rims_in,
    egrad_ref, grad_ref, head_ref,
    dpre_ref, gg_ref, ndpre_ref, own_ref, cot_ref, we_ref, ws_ref, wr_ref, win_ref, rims_ref,
    high_ref, low_ref, base_ref, sems,
):
    node_count, width = cot_in.shape
    slots = 2 * RIM + node_count
    own = slice(RIM, RIM + node_count)
    half = egrad_ref.shape[0]
    gg, dpre, we, wr, win, ndpre, ws, sums, cot, rims = start_copies(
        [
            (gg_in, gg_ref),
            (dpre_in, dpre_ref),
            (we_in, we_ref),
            (wr_in, wr_ref),
            (win_in.at[pl.ds(0, width)], win_ref),
            (ndpre_in, ndpre_ref),
            (ws_in, ws_ref),
            (own_in, own_ref),
            (cot_in, cot_ref),
            (rims_in, rims_ref),
        ],
        sems,
    )
    gg.wait()
    high, low = split2(gg_ref[...])
    for ref, part in ((high_ref, high), (low_ref, low)):
        ref[...] = jnp.zeros_like(ref)
        ref[own] = part
    rows = pl.ds(pl.multiple_of(core_ref[0] * half, half), half)
    hot = hot_rows(ids_ref[1:2, rows], 0, slots)
    upstream = dot(hot, high_ref[...]) + dot(hot, low_ref[...])
    dpre.wait()
    we.wait()
    egrad_ref[...] = (upstream + dot_t(dpre_ref[rows, :], we_ref[...])).astype(BF)
    recv = dot(hot_cols(ids_ref[1:2, :], RIM, node_count), dpre_ref[...])
    high, low = split2(recv)
    wr.wait()
    base = dot_t(high, wr_ref[...]) + dot_t(low, wr_ref[...])
    for copy in (win, ndpre, ws, sums, cot, rims):
        copy.wait()
    base += dot_t(ndpre_ref[...], win_ref[...])
    high, low = split2(own_ref[...])
    base += dot_t(high, ws_ref[...]) + dot_t(low, ws_ref[...])
    base_ref[...] = base + cot_ref[...].astype(F32)
    base_ref[:RIM] += rims_ref[RIM:].astype(F32)
    base_ref[node_count - RIM :] += rims_ref[:RIM].astype(F32)
    head_ref[...] = base_ref[: head_ref.shape[0]]
    grad_ref[...] = base_ref[...].astype(BF)


def last_kernel(hub_ref, head_ref, grad_in, out_ref, rows_ref, sum_ref, sems):
    del grad_in
    count = hub_ref.shape[0] // HUB_DEV
    sum_ref[...] = head_ref[...]
    for r in range(HUB_DEV):
        pair = hub_ref[r * count : r * count + 8]
        for k in range(8, count, 8):
            pair += hub_ref[r * count + k : r * count + k + 8]
        hub = pair[:4] + pair[4:]
        sum_ref[r : r + 1] += jnp.concatenate([hub[j : j + 1] for j in range(4)], axis=1)
    rows_ref[...] = sum_ref[...].astype(BF)
    (copy,) = start_copies([(rows_ref, out_ref.at[pl.ds(0, rows_ref.shape[0])])], sems)
    copy.wait()


def both_ways(x, step):
    count = math.prod(lax.axis_size(a) for a in SPACE)
    pairs = [
        (2 * i + c, 2 * (i + d) + c)
        for i in range(count)
        for c, d in ((0, step), (1, -step))
        if 0 <= i + d < count
    ]
    return lax.ppermute(x, ALL, pairs)


def layer(
    nodes,
    edges,
    senders,
    receivers,
    edge_proj,
    send_proj,
    recv_proj,
    edge_bias,
    edge_out,
    edge_gain,
    edge_shift,
    node_in,
    node_bias,
    node_out,
    node_gain,
    node_shift,
    node_cot,
):
    node_count, width = nodes.shape
    half = edges.shape[0]
    edge_count = 2 * half
    ny, nz, nx = (lax.axis_size(a) for a in SPACE)
    plane = ny * nx
    hub_count = plane * HUB_DEV * nz
    slots = 2 * RIM + node_count
    core = lax.axis_index("c").astype(I32)
    own_block = lax.axis_index(SPACE)
    row = lambda v: (v.reshape(1, width), VM)
    wide = lambda rows, kind=BF: pltpu.VMEM((rows, width), kind)
    square = 2 * width * width

    my_hub, my_rim = call(
        prep_kernel,
        [(core.reshape(1), SM), (nodes, HB)],
        [((nz, 8, LANES), F32, VM), ((RIM, width), BF, VM)],
        [wide(16)],
        copies=2,
    )
    rim = both_ways(my_rim, 1)
    by_z = lax.all_to_all(my_hub, "z", 0, 0)
    (spread,) = call(
        spread_kernel,
        [(by_z.reshape(nz * 8, LANES), VM)],
        [((plane, HUB_DEV * nz, width), BF, VM)],
        room=54000,
    )
    hubs = lax.all_to_all(spread, PLANE, 0, 0).reshape(hub_count, width)

    rims = lax.all_gather(rim, "c", axis=0, tiled=True)
    other = lax.ppermute(edges, "c", [(0, 1), (1, 0)])
    ids = jnp.stack([senders, receivers])
    ids = lax.all_gather(ids, "c", axis=1, tiled=True)
    block = ids[0] // node_count
    line = ids[0] - block * node_count
    hub_y, hub_zx = block // (nz * nx), block % (nz * nx)
    hub_z, hub_x = hub_zx // nx, hub_zx % nx
    hub_slot = ((hub_y * nx + hub_x) * HUB_DEV + line) * nz + hub_z
    from_own = block == own_block
    from_left = (block == own_block - 1) & (line >= node_count - RIM)
    from_right = (block == own_block + 1) & (line < RIM)
    slot = jnp.where(
        from_own,
        RIM + line,
        jnp.where(
            from_left,
            line - (node_count - RIM),
            jnp.where(from_right, RIM + node_count + line, slots + hub_slot),
        ),
    )
    near_by = from_own | from_left | from_right
    hub_sent = jnp.where(near_by | (line != core), -1, (hub_y * nx + hub_x) * nz + hub_z)
    ids = jnp.stack([slot, ids[1] - own_block * node_count + RIM, hub_sent])

    (near,) = call(
        near_kernel,
        [
            (core.reshape(1), SM), (edges, VM), (other, VM), (ids, VM), (nodes, VM), (rims, VM),
            (edge_proj, VM), (send_proj, VM), (recv_proj, VM), row(edge_bias),
        ],
        [((edge_count, width), F32, VM)],
        [wide(slots)] * 3,
        flops=square * (edge_count * 2 + 2 * slots),
        room=46000,
    )
    new_nodes, dpre, hub_sums, my_rim, own_sums, gathered_grad, node_dpre = call(
        main_kernel,
        [
            (core.reshape(1), SM), (hubs, HB), (near, HB), (edges, HB), (other, HB), (ids, VM),
            (nodes, HB), (node_cot, HB), (send_proj, HB), (edge_out, HB), (node_in, HB), (node_out, HB),
            row(edge_gain), row(edge_shift), row(node_bias), row(node_gain), row(node_shift),
        ],
        [
            ((node_count, width), BF, VM),
            ((edge_count, width), BF, HB),
            ((hub_count // 2, width), BF, HB),
            ((RIM, width), BF, VM),
            ((node_count, width), F32, HB),
            ((node_count, width), F32, HB),
            ((node_count, width), BF, HB),
        ],
        [wide(hub_count), wide(edge_count, F32), wide(edge_count)]
        + [wide(node_count)] * 2 + [wide(width)] * 2 + [wide(2 * width), wide(width)]
        + [wide(edge_count), wide(hub_count // 2), wide(node_count, F32), wide(node_count)]
        + [wide(hub_count), wide(edge_count, F32), pltpu.VMEM((edge_count, LANES), F32)]
        + [wide(slots, F32), wide(slots), wide(slots)],
        copies=14 + edge_count // MAIN_TILE,
        flops=square * (edge_count * 6 + hub_count),
        room=0,
    )

    hub_back = lax.all_to_all(hub_sums.reshape(plane, nz, width), PLANE, 0, 0)
    rim = both_ways(my_rim, -1)
    (by_z,) = call(
        gather_kernel,
        [(hub_back, HB)],
        [((nz * 4, LANES), F32, VM)],
        [pltpu.VMEM((plane, nz, width), BF)],
        copies=4,
        room=54000,
    )
    hub_back = lax.all_to_all(by_z.reshape(nz, 4, LANES), "z", 0, 0)
    hub_back = lax.all_gather(hub_back.reshape(nz * 4, LANES), "c", axis=0, tiled=True)
    rims = lax.all_gather(rim, "c", axis=0, tiled=True)
    edge_grad, node_grad, head = call(
        late_kernel,
        [
            (core.reshape(1), SM), (dpre, HB), (ids, VM), (gathered_grad, HB), (node_dpre, HB),
            (own_sums, HB), (node_cot, HB), (edge_proj, HB), (send_proj, HB), (recv_proj, HB),
            (node_in, HB), (rims, HB),
        ],
        [((half, width), BF, VM), ((node_count, width), BF, VM), ((16, width), F32, VM)],
        [wide(edge_count), wide(node_count, F32), wide(node_count), wide(node_count, F32)]
        + [wide(node_count)] + [wide(width)] * 4 + [wide(2 * RIM)] + [wide(slots)] * 2
        + [wide(node_count, F32)],
        copies=10,
        flops=square * edge_count * 2,
    )
    (node_grad,) = call(
        last_kernel,
        [(hub_back, VM), (head, VM), (node_grad, HB)],
        [((node_count, width), BF, HB)],
        [wide(16), wide(16, F32)],
        copies=1,
        room=54000,
        aliases={2: 0},
    )
    return new_nodes, node_grad, edge_grad


def solution(mesh):
    fine = Mesh(np.asarray(mesh.devices).reshape(*SHAPE, 2), ALL)
    rows, both = P(SPACE, None), P(ALL, None)
    whole = P()
    in_specs = (rows, both, P(ALL), P(ALL)) + (whole,) * 12 + (rows,)
    return jax.shard_map(
        layer, mesh=fine, in_specs=in_specs, out_specs=(rows, rows, both), check_vma=False
    )
```
